512 devices in a mesh: pix: 32 (over z, core), tm: 16 (over y, x).
Axes of the slice: x: 4, y: 4, z: 16, core: 2. Of those that a mesh axis runs over, the one named last changes fastest.
Arguments:
- raw_frames: bfloat16 [1024, 262144], P('tm', 'pix'), may hold values from 0.099609375 to 4
- eigen_flats: bfloat16 [16, 262144], P(None, 'pix'), may hold values from 0 to 1
- weights: float32 [1024, 16], P('tm'), may hold values from 0.02 to 1
- flat_count: int32 [1024], P('tm'), may hold values from 1 to 16
- bin_map: int32 [262144], P('pix'), may hold values from 0 to 64, as said below
Outputs:
- two_time: float32 [64, 1024, 1024], P('pix', 'tm')
The draws below stay inside these ranges and needn't reach their ends.
Inputs may be any that keep to these rules, and one draw needn't show every extreme that they name: `bin_map`: each block of 8192 pixels (one device's tile) holds 60 to 96 pixels of every bin 1 to 64; in every draw one bin holds exactly 96 pixels in every tile.
All inputs are finite; a program needn't handle non-finite values.
Results may differ from the reference program's by a relative error of at most 0.0003.
Values may be sent and summed in bfloat16 or wider, within the bound.
No kernel may reach another device: no remote copies, remote signals or barrier semaphores. Data moves between devices by JAX's collectives and lax.ppermute only.
A program may use at most 64 MiB of HBM per device.

```python
import math
import jax
import jax.numpy as jnp
from jax import lax

PIX_DEV = 8192
K = 16
CAP = 96
Q = 64
T_SIZE = 1024
P_SIZE = 262144
N_PIX = 32


def draw_bin_map(key, part):
    tiles = P_SIZE // PIX_DEV
    first_key, second_key, third_key = jax.random.split(jax.random.fold_in(key, 11), 3)
    lowest = CAP * 5 // 8
    counts = jax.random.randint(first_key, (tiles, Q), lowest, CAP + 1)
    full_bin = jax.random.randint(second_key, (), 0, Q)
    counts = jnp.where(jnp.arange(Q, dtype=jnp.int32)[None, :] == full_bin, CAP, counts)
    ends = jnp.cumsum(counts, axis=1)
    places = jnp.arange(PIX_DEV, dtype=jnp.int32)
    labels = 1 + jnp.sum(places[None, :, None] >= ends[:, None, :], axis=2)
    labels = jnp.where(labels > Q, 0, labels)
    tile_keys = jax.random.split(third_key, tiles)
    shuffles = jax.vmap(lambda one_key: jax.random.permutation(one_key, PIX_DEV))(tile_keys)
    mixed = jnp.take_along_axis(labels, shuffles, axis=1)
    return mixed.reshape(-1).astype(jnp.int32)


def draw_flat_count(key, part):
    first_key, second_key = jax.random.split(jax.random.fold_in(key, 23))
    counts = jax.random.randint(first_key, (T_SIZE,), 1, K + 1)
    places = jax.random.permutation(second_key, T_SIZE)
    counts = counts.at[places[0]].set(K)
    counts = counts.at[places[1]].set(1)
    return counts.astype(jnp.int32)


def block_levels(rng, shape, pieces, low, top_value):
    def one(position, shards_of):
        heights = jax.random.uniform(jax.random.fold_in(jax.random.fold_in(rng, 6), position), (shards_of,), jnp.float32, low / len(pieces), top_value / len(pieces))
        return jnp.repeat(jnp.exp(heights), shape[position] // shards_of).reshape((-1,) + (1,) * (len(shape) - position - 1))

    gain = one(*pieces[0])
    for cut in pieces[1:]:
        gain = gain * one(*cut)
    return gain


def setup_inputs(seed: int = 0) -> dict:
    keys = jax.random.split(jax.random.key(seed), 6)
    raw_frames = jnp.clip(0.099609375 + 3.9003906 * jax.random.uniform(keys[0], (T_SIZE, P_SIZE), jnp.float32) ** block_levels(keys[0], (T_SIZE, P_SIZE), ((0, 16), (1, 32)), -0.2, 0.2), 0.099609375, 4.0).astype(jnp.bfloat16)
    eigen_flats = jnp.clip(1.0 * jax.random.uniform(keys[1], (K, P_SIZE), jnp.float32) ** block_levels(keys[1], (K, P_SIZE), ((1, 32),), -0.2, 0.2), 0.0, 1.0).astype(jnp.bfloat16)
    weights = jnp.clip(jnp.exp(math.log(1.0) - 3.912023 * jax.random.uniform(keys[2], (T_SIZE, K), jnp.float32) ** block_levels(keys[2], (T_SIZE, K), ((0, 16),), -0.2, 0.2)), 0.02, 1.0)
    flat_count = draw_flat_count(jax.random.fold_in(keys[5], 71), 0)
    bin_map = draw_bin_map(jax.random.fold_in(keys[5], 71), 0)
    return {"raw_frames": raw_frames, "eigen_flats": eigen_flats, "weights": weights, "flat_count": flat_count, "bin_map": bin_map}


def reference(raw_frames, eigen_flats, weights, flat_count, bin_map):
    in_use = jnp.arange(K, dtype=jnp.int32)[None, :] < flat_count[:, None]
    coefficients = jnp.where(in_use, weights, 0.0)
    flat_field = 0.5 + jnp.dot(coefficients, eigen_flats.astype(jnp.float32), precision=lax.Precision.HIGHEST)
    corrected = (raw_frames.astype(jnp.float32) / flat_field).astype(jnp.bfloat16)
    pixels = bin_map.shape[0]
    labels = jnp.where(bin_map > 0, bin_map - 1, Q).astype(jnp.int32)
    ordering = jnp.argsort(labels * pixels + jnp.arange(pixels, dtype=jnp.int32)).astype(jnp.int32)
    member_counts = jnp.sum(labels[:, None] == jnp.arange(Q, dtype=jnp.int32)[None, :], axis=0).astype(jnp.int32)
    starts = jnp.cumsum(member_counts).astype(jnp.int32) - member_counts
    slot_index = jnp.arange(N_PIX * CAP, dtype=jnp.int32)

    def one_bin(index):
        first = starts[index]
        total = member_counts[index]
        columns = ordering[jnp.minimum(first + slot_index, pixels - 1)]
        chosen = jnp.where((slot_index < total)[None, :], corrected[:, columns], jnp.zeros((), jnp.bfloat16))
        products = jnp.dot(chosen, chosen.T, preferred_element_type=jnp.float32)
        sums = jnp.sum(chosen, axis=1, dtype=jnp.float32)
        scaled = total.astype(jnp.float32) * products
        return scaled / (sums[:, None] * sums[None, :])

    return lax.map(one_bin, jnp.arange(Q, dtype=jnp.int32))
```

```python
import jax, jax.numpy as jnp
from jax import lax
from jax.experimental import pallas as pl
from jax.experimental.pallas import tpu as pltpu
from jax.sharding import Mesh, PartitionSpec as P

CAP = 96
FRAMES = 64
PIXELS = 8192
EIGEN = 16
BINS = 64
CHUNK = 256
CHUNKS = PIXELS // CHUNK
SLOTS = BINS * CAP
PART = 24
DESTS = 128
DEPTH = 32 * PART


def pack_kernel(coef_ref, bins_ref, eigen_ref, raw_ref, out_ref,
                hot_ref, cum_ref, row_ref, place_ref, even_ref, odd_ref, slot_ref, sem):
    f32, bf16 = jnp.float32, jnp.bfloat16
    label = lax.broadcasted_iota(jnp.int32, (BINS, CHUNK), 0) + 1
    for j in range(CHUNKS):
        hot_ref[j * BINS:(j + 1) * BINS, :] = jnp.where(
            bins_ref[j:j + 1, :] == label, 1.0, 0.0).astype(bf16)
    before = lax.broadcasted_iota(jnp.int32, (CHUNK, CHUNK + 128), 0)
    after = lax.broadcasted_iota(jnp.int32, (CHUNK, CHUNK + 128), 1)
    prefix = jnp.where((before < after) | (after >= CHUNK), 1.0, 0.0).astype(bf16)
    cum_ref[...] = jnp.dot(hot_ref[...], prefix, preferred_element_type=f32)
    carry = jnp.zeros((BINS, 128), f32)
    for j in range(CHUNKS):
        rows = slice(j * BINS, (j + 1) * BINS)
        for h in range(2):
            lanes = slice(h * 128, (h + 1) * 128)
            rank = jnp.sum(hot_ref[rows, lanes].astype(f32) * (cum_ref[rows, lanes] + carry), axis=0, keepdims=True)
            own = bins_ref[j:j + 1, lanes]
            row_ref[2 * j + h:2 * j + h + 1, :] = jnp.where(
                own > 0, (own - 1) * CAP + rank.astype(jnp.int32), SLOTS)
        carry = carry + cum_ref[rows, CHUNK:]
    copy = pltpu.make_async_copy(row_ref, place_ref, sem)
    copy.start()

    zero = jnp.zeros((128, 128), f32)

    @pl.loop(0, SLOTS // 128)
    def _(i):
        slot_ref[pl.ds(pl.multiple_of(i * 128, 128), 128), :] = zero
    slot_ref[SLOTS:, :] = jnp.zeros((8, 128), f32)

    coef = coef_ref[...]
    high = coef.astype(bf16)
    rest = coef - high.astype(f32)
    mid = rest.astype(bf16)
    low = (rest - mid.astype(f32)).astype(bf16)
    weights = jnp.concatenate([high, mid, low], axis=1)

    def correct(j, target):
        at = pl.ds(pl.multiple_of(j * CHUNK, CHUNK), CHUNK)
        flats = eigen_ref[:, at]
        field = 0.5 + jnp.dot(weights, jnp.concatenate([flats] * 3, axis=0), preferred_element_type=f32)
        value = (raw_ref[:, at].astype(f32) / field).astype(bf16).astype(f32)
        for h in range(2):
            half = value[:, h * 128:(h + 1) * 128]
            target[h * 128:(h + 1) * 128, :] = jnp.concatenate([half, half], axis=0).T

    def scatter(j, source):
        for h in range(2):
            for i in range(128):
                place = place_ref[2 * j + h, i]
                slot_ref[pl.ds(place, 1), :] = source[h * 128 + i:h * 128 + i + 1, :]

    correct(0, even_ref)
    copy.wait()

    @pl.loop(0, CHUNKS // 2 - 1)
    def _(i):
        scatter(2 * i, even_ref)
        correct(2 * i + 1, odd_ref)
        scatter(2 * i + 1, odd_ref)
        correct(2 * i + 2, even_ref)
    scatter(CHUNKS - 2, even_ref)
    correct(CHUNKS - 1, odd_ref)
    scatter(CHUNKS - 1, odd_ref)

    left = lax.broadcasted_iota(jnp.int32, (PART, 128), 1) < FRAMES

    @pl.loop(0, BINS // 4)
    def _(z):
        for x in range(4):
            for c in range(2):
                base = (4 * z + x) * CAP + c * 2 * PART
                lo = slot_ref[pl.ds(pl.multiple_of(base, 8), PART), :]
                hi = slot_ref[pl.ds(pl.multiple_of(base + PART, 8), PART), :]
                out_ref[x * 32 + 2 * z + c] = jnp.where(left, lo, hi).astype(bf16)


def pack(coef, bins, eigen, raw):
    f32 = jnp.float32
    return pl.pallas_call(
        pack_kernel,
        out_shape=jax.ShapeDtypeStruct((DESTS, PART, 128), jnp.bfloat16),
        in_specs=[pl.BlockSpec(memory_space=pltpu.VMEM)] * 4,
        out_specs=pl.BlockSpec(memory_space=pltpu.VMEM),
        scratch_shapes=[
            pltpu.VMEM((CHUNKS * BINS, CHUNK), jnp.bfloat16),
            pltpu.VMEM((CHUNKS * BINS, CHUNK + 128), f32),
            pltpu.VMEM((PIXELS // 128, 128), jnp.int32),
            pltpu.SMEM((PIXELS // 128, 128), jnp.int32),
            pltpu.VMEM((CHUNK, 128), f32),
            pltpu.VMEM((CHUNK, 128), f32),
            pltpu.VMEM((SLOTS + 8, 128), f32),
            pltpu.SemaphoreType.DMA,
        ],
        compiler_params=pltpu.CompilerParams(vmem_limit_bytes=40 << 20),
        name="pack",
    )(coef, bins, eigen, raw)


def gram_kernel(core_ref, mine_ref, next_ref, last_ref, keep_ref, send_ref, own_ref):
    f32, bf16 = jnp.float32, jnp.bfloat16
    first = core_ref[0] == 0
    left = lax.broadcasted_iota(jnp.int32, (1, 128), 1) < FRAMES
    ones = jnp.ones((8, DEPTH), bf16)

    def matrix(ref):
        return jnp.concatenate([ref[x * DEPTH:(x + 1) * DEPTH, :] for x in range(4)], axis=1)

    def fold(even_top, even_low, odd_top, odd_low):
        return jnp.where(left, even_top, odd_low) + pltpu.roll(
            jnp.where(left, odd_top, even_low), FRAMES, 1)

    def product(a, b, group):
        full = lax.dot_general(a, b, (((0,), (0,)), ((), ())), preferred_element_type=f32)
        for x in range(4):
            top, low = slice(x * 128, x * 128 + 64), slice(x * 128 + 64, x * 128 + 128)
            for e in range(2):
                even, odd = slice(e * 256, e * 256 + 128), slice(e * 256 + 128, e * 256 + 256)
                part = fold(full[top, even], full[low, even], full[top, odd], full[low, odd])
                lanes = slice(group * 256 + e * 128, group * 256 + e * 128 + 128)
                keep_ref[x, :, lanes] = jnp.where(first, part[:32], part[32:])
                send_ref[x * 32:(x + 1) * 32, lanes] = jnp.where(first, part[32:], part[:32])

    def total(b, group):
        full = jnp.dot(ones, b, preferred_element_type=f32)
        for e in range(2):
            even, odd = full[:, e * 256:e * 256 + 128], full[:, e * 256 + 128:e * 256 + 256]
            lanes = slice(group * 256 + e * 128, group * 256 + e * 128 + 128)
            part = fold(even, even, odd, odd)
            own_ref[:, lanes] = part
            send_ref[128:, lanes] = part

    mine, after, prior = matrix(mine_ref), matrix(next_ref), matrix(last_ref)
    product(mine, mine, 1)
    product(mine, prior, 0)
    product(mine, after, 2)
    product(prior, after, 3)
    total(prior, 0)
    total(mine, 1)
    total(after, 2)
    hits = jnp.where(mine_ref[:DEPTH, :].astype(f32) != 0.0, 1.0, 0.0).astype(bf16)
    hits = jnp.dot(ones, hits, preferred_element_type=f32)
    hits = hits + pltpu.roll(hits, FRAMES, 1)
    for e in range(2):
        own_ref[:, 768 + e * 128:896 + e * 128] = hits
        send_ref[128:, 768 + e * 128:896 + e * 128] = hits


def gram(core, mine, after, prior):
    f32 = jnp.float32
    return pl.pallas_call(
        gram_kernel,
        out_shape=(jax.ShapeDtypeStruct((4, 32, 1024), f32),
                   jax.ShapeDtypeStruct((136, 1024), f32),
                   jax.ShapeDtypeStruct((8, 1024), f32)),
        in_specs=[pl.BlockSpec(memory_space=pltpu.SMEM)] + [pl.BlockSpec(memory_space=pltpu.VMEM)] * 3,
        out_specs=(pl.BlockSpec(memory_space=pltpu.VMEM),) * 3,
        compiler_params=pltpu.CompilerParams(vmem_limit_bytes=40 << 20),
        name="gram",
    )(core, mine, after, prior)


def scale_kernel(core_ref, keep_ref, got_ref, own_ref, rows_ref, far_ref):
    first = core_ref[0] == 0
    sums = own_ref[...] + got_ref[128:, :]
    count = sums[0:1, 768:896]
    count = jnp.concatenate([count, count], axis=1)

    def column(group):
        tall = [jnp.broadcast_to(sums[0:1, group * 256 + e * 128:group * 256 + e * 128 + 128], (128, 128)).T
                for e in range(2)]
        tall = jnp.concatenate(tall, axis=0)
        parts = []
        for x in range(4):
            part = jnp.where(first, tall[x * 64:x * 64 + 32], tall[x * 64 + 32:x * 64 + 64])
            parts.append(jnp.concatenate([part, part], axis=1))
        return parts

    mine, prior = column(1), column(0)
    for x in range(4):
        for group in range(4):
            lanes = slice(group * 256, group * 256 + 256)
            value = keep_ref[x, :, lanes] + got_ref[x * 32:(x + 1) * 32, lanes]
            if group < 3:
                rows_ref[x, :, lanes] = count * value / (mine[x] * sums[0:1, lanes])
            else:
                far_ref[x] = count * value / (prior[x] * sums[0:1, 512:768])


def scale(core, keep, got, own):
    f32 = jnp.float32
    return pl.pallas_call(
        scale_kernel,
        out_shape=(jax.ShapeDtypeStruct((4, 32, 768), f32),
                   jax.ShapeDtypeStruct((4, 32, 256), f32)),
        in_specs=[pl.BlockSpec(memory_space=pltpu.SMEM)] + [pl.BlockSpec(memory_space=pltpu.VMEM)] * 3,
        out_specs=(pl.BlockSpec(memory_space=pltpu.VMEM),) * 2,
        name="scale",
    )(core, keep, got, own)


def place_kernel(at_ref, rows_ref, got_ref, out_ref):
    core, row = at_ref[0], at_ref[1]
    for b in range(2):
        for group in range(4):
            lanes = pl.ds(pl.multiple_of(lax.rem(row + 3 + group, 4) * 256, 256), 256)
            out_ref[b, pl.ds(pl.multiple_of(core * 32, 32), 32), lanes] = (
                rows_ref[2 * core + b, :, group * 256:(group + 1) * 256])
            out_ref[b, pl.ds(pl.multiple_of((1 - core) * 32, 32), 32), lanes] = (
                got_ref[b, :, group * 256:(group + 1) * 256])


def place(at, rows, got):
    return pl.pallas_call(
        place_kernel,
        out_shape=jax.ShapeDtypeStruct((2, 64, 1024), jnp.float32),
        in_specs=[pl.BlockSpec(memory_space=pltpu.SMEM)] + [pl.BlockSpec(memory_space=pltpu.VMEM)] * 2,
        out_specs=pl.BlockSpec(memory_space=pltpu.VMEM),
        name="place",
    )(at, rows, got)


def shift(size, step):
    return [(i, (i + step) % size) for i in range(size)]


def shards(raw_frames, eigen_flats, weights, flat_count, bin_map):
    core = lax.axis_index("c").astype(jnp.int32)
    row = lax.axis_index("y").astype(jnp.int32)
    in_use = lax.broadcasted_iota(jnp.int32, (FRAMES, EIGEN), 1) < flat_count[:, None]
    coefficients = jnp.where(in_use, weights, 0.0)
    packed = pack(coefficients, bin_map.reshape(CHUNKS, CHUNK), eigen_flats, raw_frames)
    mine = lax.all_to_all(packed, ("x", "z", "c"), 0, 0, tiled=True).reshape(4 * DEPTH, 128)
    prior = lax.ppermute(mine, "y", shift(4, 1))
    after = lax.ppermute(mine, "y", shift(4, -1))
    keep, send, own = gram(core[None], mine, after, prior)
    got = lax.ppermute(send, "c", shift(2, 1))
    rows, far = scale(core[None], keep, got, own)
    far = lax.ppermute(far, "y", shift(4, -1))
    rows = lax.all_to_all(jnp.concatenate([rows, far], axis=2), "x", 0, 0, tiled=True)
    other = lax.ppermute(lax.dynamic_slice_in_dim(rows, 2 * (1 - core), 2, 0), "c", shift(2, 1))
    return place(jnp.stack([core, row]), rows, other)


def solution(mesh):
    split = Mesh(mesh.devices.reshape(16, 2, 4, 4), ("z", "c", "y", "x"))
    return jax.shard_map(
        shards,
        mesh=split,
        in_specs=(P(("y", "x"), ("z", "c")), P(None, ("z", "c")), P(("y", "x"), None), P(("y", "x")), P(("z", "c"))),
        out_specs=P(("z", "c"), ("y", "x"), None),
        check_vma=False,
    )
```

```python
import jax, jax.numpy as jnp
from jax import lax
from jax.experimental import pallas as pl
from jax.experimental.pallas import tpu as pltpu
from jax.sharding import Mesh, PartitionSpec as P

CAP = 96
FRAMES = 64
PIXELS = 8192
EIGEN = 16
BINS = 64
CHUNK = 256
CHUNKS = PIXELS // CHUNK
SLOTS = BINS * CAP
PART = 24
DESTS = 128
DEPTH = 32 * PART


def pack_kernel(weights_hbm, used_hbm, bins_hbm, eigen_hbm, raw_hbm, out_ref,
                weights_ref, used_ref, bins_ref, eigen_ref, raw_ref,
                hot_ref, cum_ref, row_ref, place_ref, even_ref, odd_ref, slot_ref, sems):
    f32, bf16 = jnp.float32, jnp.bfloat16
    sources = (bins_hbm, eigen_hbm, weights_hbm, used_hbm, raw_hbm)
    targets = (bins_ref, eigen_ref, weights_ref, used_ref, raw_ref)
    loads = [pltpu.make_async_copy(a, b, sems.at[i]) for i, (a, b) in enumerate(zip(sources, targets))]
    for load in loads:
        load.start()
    zero = jnp.zeros((128, 128), f32)

    @pl.loop(0, SLOTS // 128)
    def _(i):
        slot_ref[pl.ds(pl.multiple_of(i * 128, 128), 128), :] = zero
    slot_ref[SLOTS:, :] = jnp.zeros((8, 128), f32)
    loads[0].wait()

    label = lax.broadcasted_iota(jnp.int32, (BINS, 128), 0) + 1
    for j in range(CHUNKS):
        for h in range(2):
            hot_ref[j * BINS:(j + 1) * BINS, h * 128:(h + 1) * 128] = jnp.where(
                bins_ref[2 * j + h:2 * j + h + 1, :] == label, 1.0, 0.0).astype(bf16)
    before = lax.broadcasted_iota(jnp.int32, (CHUNK, CHUNK + 128), 0)
    after = lax.broadcasted_iota(jnp.int32, (CHUNK, CHUNK + 128), 1)
    prefix = jnp.where((before < after) | (after >= CHUNK), 1.0, 0.0).astype(bf16)
    cum_ref[...] = jnp.dot(hot_ref[...], prefix, preferred_element_type=f32)
    carry = jnp.zeros((BINS, 128), f32)
    for j in range(CHUNKS):
        rows = slice(j * BINS, (j + 1) * BINS)
        for h in range(2):
            lanes = slice(h * 128, (h + 1) * 128)
            rank = jnp.sum(hot_ref[rows, lanes].astype(f32) * (cum_ref[rows, lanes] + carry), axis=0, keepdims=True)
            own = bins_ref[2 * j + h:2 * j + h + 1, :]
            row_ref[2 * j + h:2 * j + h + 1, :] = jnp.where(
                own > 0, (own - 1) * CAP + rank.astype(jnp.int32), SLOTS)
        carry = carry + cum_ref[rows, CHUNK:]
    copy = pltpu.make_async_copy(row_ref, place_ref, sems.at[5])
    copy.start()
    for load in loads[1:]:
        load.wait()

    in_use = lax.broadcasted_iota(jnp.int32, (EIGEN, FRAMES), 0) < used_ref[...]
    coef = jnp.where(in_use, weights_ref[...], 0.0)
    high = coef.astype(bf16)
    rest = coef - high.astype(f32)
    mid = rest.astype(bf16)
    low = (rest - mid.astype(f32)).astype(bf16)
    weights = jnp.concatenate([high.astype(f32), mid.astype(f32), low.astype(f32)], axis=0).T.astype(bf16)

    def correct(j, target):
        at = pl.ds(pl.multiple_of(j * CHUNK, CHUNK), CHUNK)
        flats = eigen_ref[:, at]
        field = 0.5 + jnp.dot(weights, jnp.concatenate([flats] * 3, axis=0), preferred_element_type=f32)
        value = (raw_ref[:, at].astype(f32) / field).astype(bf16).astype(f32)
        for h in range(2):
            half = value[:, h * 128:(h + 1) * 128]
            target[h * 128:(h + 1) * 128, :] = jnp.concatenate([half, half], axis=0).T

    def scatter(j, source):
        for h in range(2):
            for i in range(128):
                place = place_ref[2 * j + h, i]
                slot_ref[pl.ds(place, 1), :] = source[h * 128 + i:h * 128 + i + 1, :]

    correct(0, even_ref)
    copy.wait()

    @pl.loop(0, CHUNKS // 2 - 1)
    def _(i):
        scatter(2 * i, even_ref)
        correct(2 * i + 1, odd_ref)
        scatter(2 * i + 1, odd_ref)
        correct(2 * i + 2, even_ref)
    scatter(CHUNKS - 2, even_ref)
    correct(CHUNKS - 1, odd_ref)
    scatter(CHUNKS - 1, odd_ref)

    left = lax.broadcasted_iota(jnp.int32, (PART, 128), 1) < FRAMES

    @pl.loop(0, BINS // 4)
    def _(z):
        for x in range(4):
            for c in range(2):
                base = (4 * z + x) * CAP + c * 2 * PART
                lo = slot_ref[pl.ds(pl.multiple_of(base, 8), PART), :]
                hi = slot_ref[pl.ds(pl.multiple_of(base + PART, 8), PART), :]
                out_ref[x * 32 + 2 * z + c] = jnp.where(left, lo, hi).astype(bf16)


def pack(weights, used, bins, eigen, raw):
    f32 = jnp.float32
    return pl.pallas_call(
        pack_kernel,
        out_shape=jax.ShapeDtypeStruct((DESTS, PART, 128), jnp.bfloat16),
        in_specs=[pl.BlockSpec(memory_space=pltpu.HBM)] * 5,
        out_specs=pl.BlockSpec(memory_space=pltpu.VMEM),
        scratch_shapes=[
            pltpu.VMEM((EIGEN, FRAMES), f32),
            pltpu.VMEM((1, FRAMES), jnp.int32),
            pltpu.VMEM((PIXELS // 128, 128), jnp.int32),
            pltpu.VMEM((EIGEN, PIXELS), jnp.bfloat16),
            pltpu.VMEM((FRAMES, PIXELS), jnp.bfloat16),
            pltpu.VMEM((CHUNKS * BINS, CHUNK), jnp.bfloat16),
            pltpu.VMEM((CHUNKS * BINS, CHUNK + 128), f32),
            pltpu.VMEM((PIXELS // 128, 128), jnp.int32),
            pltpu.SMEM((PIXELS // 128, 128), jnp.int32),
            pltpu.VMEM((CHUNK, 128), f32),
            pltpu.VMEM((CHUNK, 128), f32),
            pltpu.VMEM((SLOTS + 8, 128), f32),
            pltpu.SemaphoreType.DMA((6,)),
        ],
        compiler_params=pltpu.CompilerParams(vmem_limit_bytes=24 << 20),
        name="pack",
    )(*(pltpu.with_memory_space_constraint(a, pltpu.HBM) for a in (weights, used, bins, eigen, raw)))


def gram_kernel(core_ref, mine_ref, next_ref, last_ref, keep_ref, send_ref, own_ref):
    f32, bf16 = jnp.float32, jnp.bfloat16
    first = core_ref[0] == 0
    left = lax.broadcasted_iota(jnp.int32, (1, 128), 1) < FRAMES
    ones = jnp.ones((8, DEPTH), bf16)

    def matrix(ref):
        return jnp.concatenate([ref[x * DEPTH:(x + 1) * DEPTH, :] for x in range(4)], axis=1)

    def fold(even_top, even_low, odd_top, odd_low):
        return jnp.where(left, even_top, odd_low) + pltpu.roll(
            jnp.where(left, odd_top, even_low), FRAMES, 1)

    def product(a, b, group):
        full = lax.dot_general(a, b, (((0,), (0,)), ((), ())), preferred_element_type=f32)
        for x in range(4):
            top, low = slice(x * 128, x * 128 + 64), slice(x * 128 + 64, x * 128 + 128)
            for e in range(2):
                even, odd = slice(e * 256, e * 256 + 128), slice(e * 256 + 128, e * 256 + 256)
                part = fold(full[top, even], full[low, even], full[top, odd], full[low, odd])
                lanes = slice(group * 256 + e * 128, group * 256 + e * 128 + 128)
                keep_ref[x, :, lanes] = jnp.where(first, part[:32], part[32:])
                send_ref[x * 32:(x + 1) * 32, lanes] = jnp.where(first, part[32:], part[:32])

    def total(b, group):
        full = jnp.dot(ones, b, preferred_element_type=f32)
        for e in range(2):
            even, odd = full[:, e * 256:e * 256 + 128], full[:, e * 256 + 128:e * 256 + 256]
            lanes = slice(group * 256 + e * 128, group * 256 + e * 128 + 128)
            part = fold(even, even, odd, odd)
            own_ref[:, lanes] = part
            send_ref[128:, lanes] = part

    mine, after, prior = matrix(mine_ref), matrix(next_ref), matrix(last_ref)
    product(mine, mine, 1)
    product(mine, prior, 0)
    product(mine, after, 2)
    product(prior, after, 3)
    total(prior, 0)
    total(mine, 1)
    total(after, 2)
    hits = jnp.where(mine_ref[:DEPTH, :].astype(f32) != 0.0, 1.0, 0.0).astype(bf16)
    hits = jnp.dot(ones, hits, preferred_element_type=f32)
    hits = hits + pltpu.roll(hits, FRAMES, 1)
    for e in range(2):
        own_ref[:, 768 + e * 128:896 + e * 128] = hits
        send_ref[128:, 768 + e * 128:896 + e * 128] = hits


def gram(core, mine, after, prior):
    f32 = jnp.float32
    return pl.pallas_call(
        gram_kernel,
        out_shape=(jax.ShapeDtypeStruct((4, 32, 1024), f32),
                   jax.ShapeDtypeStruct((136, 1024), f32),
                   jax.ShapeDtypeStruct((8, 1024), f32)),
        in_specs=[pl.BlockSpec(memory_space=pltpu.SMEM)] + [pl.BlockSpec(memory_space=pltpu.VMEM)] * 3,
        out_specs=(pl.BlockSpec(memory_space=pltpu.VMEM),) * 3,
        compiler_params=pltpu.CompilerParams(vmem_limit_bytes=24 << 20),
        name="gram",
    )(core, mine, after, prior)


def scale_kernel(core_ref, keep_ref, got_ref, own_ref, rows_ref, far_ref):
    first = core_ref[0] == 0
    sums = own_ref[...] + got_ref[128:, :]
    count = sums[0:1, 768:896]
    count = jnp.concatenate([count, count], axis=1)

    def column(group):
        tall = [jnp.broadcast_to(sums[0:1, group * 256 + e * 128:group * 256 + e * 128 + 128], (128, 128)).T
                for e in range(2)]
        tall = jnp.concatenate(tall, axis=0)
        parts = []
        for x in range(4):
            part = jnp.where(first, tall[x * 64:x * 64 + 32], tall[x * 64 + 32:x * 64 + 64])
            parts.append(jnp.concatenate([part, part], axis=1))
        return parts

    mine, prior = column(1), column(0)
    for x in range(4):
        for group in range(4):
            lanes = slice(group * 256, group * 256 + 256)
            value = keep_ref[x, :, lanes] + got_ref[x * 32:(x + 1) * 32, lanes]
            if group < 3:
                rows_ref[x, :, lanes] = count * value / (mine[x] * sums[0:1, lanes])
            else:
                value = count * value / (prior[x] * sums[0:1, 512:768])
                rows_ref[x, :, lanes] = value
                far_ref[x] = value


def scale(core, keep, got, own):
    f32 = jnp.float32
    return pl.pallas_call(
        scale_kernel,
        out_shape=(jax.ShapeDtypeStruct((4, 32, 1024), f32),
                   jax.ShapeDtypeStruct((4, 32, 256), f32)),
        in_specs=[pl.BlockSpec(memory_space=pltpu.SMEM)] + [pl.BlockSpec(memory_space=pltpu.VMEM)] * 3,
        out_specs=(pl.BlockSpec(memory_space=pltpu.VMEM),) * 2,
        compiler_params=pltpu.CompilerParams(vmem_limit_bytes=8 << 20),
        name="scale",
    )(core, keep, got, own)


def place_kernel(at_ref, rows_ref, got_ref, out_ref):
    core, row = at_ref[0], at_ref[1]
    for b in range(2):
        for group in range(4):
            lanes = pl.ds(pl.multiple_of(lax.rem(row + 3 + group, 4) * 256, 256), 256)
            out_ref[b, pl.ds(pl.multiple_of(core * 32, 32), 32), lanes] = (
                rows_ref[2 * core + b, :, group * 256:(group + 1) * 256])
            out_ref[b, pl.ds(pl.multiple_of((1 - core) * 32, 32), 32), lanes] = (
                got_ref[b, :, group * 256:(group + 1) * 256])


def place(at, rows, got):
    return pl.pallas_call(
        place_kernel,
        out_shape=jax.ShapeDtypeStruct((2, 64, 1024), jnp.float32),
        in_specs=[pl.BlockSpec(memory_space=pltpu.SMEM)] + [pl.BlockSpec(memory_space=pltpu.VMEM)] * 2,
        out_specs=pl.BlockSpec(memory_space=pltpu.VMEM),
        compiler_params=pltpu.CompilerParams(vmem_limit_bytes=8 << 20),
        name="place",
    )(at, rows, got)


def shift(size, step):
    return [(i, (i + step) % size) for i in range(size)]


def shards(raw_frames, eigen_flats, weights, flat_count, bin_map):
    core = lax.axis_index("c").astype(jnp.int32)
    row = lax.axis_index("y").astype(jnp.int32)
    packed = pack(weights.T, flat_count[None, :], bin_map.reshape(PIXELS // 128, 128), eigen_flats, raw_frames)
    mine = lax.all_to_all(packed, ("x", "z", "c"), 0, 0, tiled=True).reshape(4 * DEPTH, 128)
    prior = lax.ppermute(mine, "y", shift(4, 1))
    after = lax.ppermute(mine, "y", shift(4, -1))
    keep, send, own = gram(core[None], mine, after, prior)
    got = lax.ppermute(send, "c", shift(2, 1))
    rows, far = scale(core[None], keep, got, own)
    far = lax.ppermute(far, "y", shift(4, -1))
    rows = lax.all_to_all(rows.at[:, :, 768:].set(far), "x", 0, 0, tiled=True)
    other = lax.ppermute(lax.dynamic_slice_in_dim(rows, 2 * (1 - core), 2, 0), "c", shift(2, 1))
    return place(jnp.stack([core, row]), rows, other)


def solution(mesh):
    split = Mesh(mesh.devices.reshape(16, 2, 4, 4), ("z", "c", "y", "x"))
    return jax.shard_map(
        shards,
        mesh=split,
        in_specs=(P(("y", "x"), ("z", "c")), P(None, ("z", "c")), P(("y", "x"), None), P(("y", "x")), P(("z", "c"))),
        out_specs=P(("z", "c"), ("y", "x"), None),
        check_vma=False,
    )
```

```python
import jax, jax.numpy as jnp
from jax import lax
from jax.experimental import pallas as pl
from jax.experimental.pallas import tpu as pltpu
from jax.sharding import Mesh, PartitionSpec as P

CAP = 96
FRAMES = 64
PIXELS = 8192
EIGEN = 16
BINS = 64
CHUNK = 256
CHUNKS = PIXELS // CHUNK
SLOTS = BINS * CAP
PART = 24
DESTS = 128
DEPTH = 32 * PART


def pack_kernel(weights_hbm, used_hbm, bins_hbm, eigen_hbm, raw_hbm, out_ref,
                weights_ref, used_ref, bins_ref, eigen_ref, raw_ref,
                hot_ref, cum_ref, row_ref, place_ref, even_ref, odd_ref, slot_ref, sems):
    f32, bf16 = jnp.float32, jnp.bfloat16
    sources = (bins_hbm, eigen_hbm, weights_hbm, used_hbm, raw_hbm)
    targets = (bins_ref, eigen_ref, weights_ref, used_ref, raw_ref)
    loads = [pltpu.make_async_copy(a, b, sems.at[i]) for i, (a, b) in enumerate(zip(sources, targets))]
    for load in loads:
        load.start()
    zero = jnp.zeros((128, 128), f32)

    @pl.loop(0, SLOTS // 128)
    def _(i):
        slot_ref[pl.ds(pl.multiple_of(i * 128, 128), 128), :] = zero
    slot_ref[SLOTS:, :] = jnp.zeros((8, 128), f32)
    loads[0].wait()

    label = lax.broadcasted_iota(jnp.int32, (BINS, 128), 0) + 1
    for j in range(CHUNKS):
        for h in range(2):
            hot_ref[j * BINS:(j + 1) * BINS, h * 128:(h + 1) * 128] = jnp.where(
                bins_ref[2 * j + h:2 * j + h + 1, :] == label, 1.0, 0.0).astype(bf16)
    before = lax.broadcasted_iota(jnp.int32, (CHUNK, CHUNK + 128), 0)
    after = lax.broadcasted_iota(jnp.int32, (CHUNK, CHUNK + 128), 1)
    prefix = jnp.where((before < after) | (after >= CHUNK), 1.0, 0.0).astype(bf16)
    cum_ref[...] = jnp.dot(hot_ref[...], prefix, preferred_element_type=f32)
    carry = jnp.zeros((BINS, 128), f32)
    for j in range(CHUNKS):
        rows = slice(j * BINS, (j + 1) * BINS)
        for h in range(2):
            lanes = slice(h * 128, (h + 1) * 128)
            rank = jnp.sum(hot_ref[rows, lanes].astype(f32) * (cum_ref[rows, lanes] + carry), axis=0, keepdims=True)
            own = bins_ref[2 * j + h:2 * j + h + 1, :]
            row_ref[2 * j + h:2 * j + h + 1, :] = jnp.where(
                own > 0, (own - 1) * CAP + rank.astype(jnp.int32), SLOTS)
        carry = carry + cum_ref[rows, CHUNK:]
    copy = pltpu.make_async_copy(row_ref, place_ref, sems.at[5])
    copy.start()
    for load in loads[1:]:
        load.wait()

    in_use = lax.broadcasted_iota(jnp.int32, (EIGEN, FRAMES), 0) < used_ref[...]
    coef = jnp.where(in_use, weights_ref[...], 0.0)
    high = coef.astype(bf16)
    rest = coef - high.astype(f32)
    mid = rest.astype(bf16)
    low = (rest - mid.astype(f32)).astype(bf16)
    weights = jnp.concatenate([high.astype(f32), mid.astype(f32), low.astype(f32)], axis=0).T.astype(bf16)

    def correct(j, target):
        at = pl.ds(pl.multiple_of(j * CHUNK, CHUNK), CHUNK)
        flats = eigen_ref[:, at]
        field = 0.5 + jnp.dot(weights, jnp.concatenate([flats] * 3, axis=0), preferred_element_type=f32)
        value = (raw_ref[:, at].astype(f32) / field).astype(bf16).astype(f32)
        for h in range(2):
            half = value[:, h * 128:(h + 1) * 128]
            target[h * 128:(h + 1) * 128, :] = jnp.concatenate([half, half], axis=0).T

    def scatter(j, source):
        for h in range(2):
            for i in range(128):
                place = place_ref[2 * j + h, i]
                slot_ref[pl.ds(place, 1), :] = source[h * 128 + i:h * 128 + i + 1, :]

    correct(0, even_ref)
    copy.wait()

    @pl.loop(0, CHUNKS // 2 - 1)
    def _(i):
        scatter(2 * i, even_ref)
        correct(2 * i + 1, odd_ref)
        scatter(2 * i + 1, odd_ref)
        correct(2 * i + 2, even_ref)
    scatter(CHUNKS - 2, even_ref)
    correct(CHUNKS - 1, odd_ref)
    scatter(CHUNKS - 1, odd_ref)

    left = lax.broadcasted_iota(jnp.int32, (PART, 128), 1) < FRAMES

    @pl.loop(0, BINS // 4)
    def _(z):
        for x in range(4):
            for c in range(2):
                base = (4 * z + x) * CAP + c * 2 * PART
                lo = slot_ref[pl.ds(pl.multiple_of(base, 8), PART), :]
                hi = slot_ref[pl.ds(pl.multiple_of(base + PART, 8), PART), :]
                out_ref[x * 32 + 2 * z + c] = jnp.where(left, lo, hi).astype(bf16)


def pack(weights, used, bins, eigen, raw):
    f32 = jnp.float32
    return pl.pallas_call(
        pack_kernel,
        out_shape=jax.ShapeDtypeStruct((DESTS, PART, 128), jnp.bfloat16),
        in_specs=[pl.BlockSpec(memory_space=pltpu.HBM)] * 5,
        out_specs=pl.BlockSpec(memory_space=pltpu.VMEM),
        scratch_shapes=[
            pltpu.VMEM((EIGEN, FRAMES), f32),
            pltpu.VMEM((1, FRAMES), jnp.int32),
            pltpu.VMEM((PIXELS // 128, 128), jnp.int32),
            pltpu.VMEM((EIGEN, PIXELS), jnp.bfloat16),
            pltpu.VMEM((FRAMES, PIXELS), jnp.bfloat16),
            pltpu.VMEM((CHUNKS * BINS, CHUNK), jnp.bfloat16),
            pltpu.VMEM((CHUNKS * BINS, CHUNK + 128), f32),
            pltpu.VMEM((PIXELS // 128, 128), jnp.int32),
            pltpu.SMEM((PIXELS // 128, 128), jnp.int32),
            pltpu.VMEM((CHUNK, 128), f32),
            pltpu.VMEM((CHUNK, 128), f32),
            pltpu.VMEM((SLOTS + 8, 128), f32),
            pltpu.SemaphoreType.DMA((6,)),
        ],
        compiler_params=pltpu.CompilerParams(vmem_limit_bytes=24 << 20),
        name="pack",
    )(*(pltpu.with_memory_space_constraint(a, pltpu.HBM) for a in (weights, used, bins, eigen, raw)))


def gram_kernel(core_ref, mine_ref, next_ref, last_ref, keep_ref, send_ref, own_ref):
    f32, bf16 = jnp.float32, jnp.bfloat16
    first = core_ref[0] == 0
    left = lax.broadcasted_iota(jnp.int32, (1, 128), 1) < FRAMES
    ones = jnp.ones((8, DEPTH), bf16)

    def matrix(ref):
        return jnp.concatenate([ref[x * DEPTH:(x + 1) * DEPTH, :] for x in range(4)], axis=1)

    def fold(even_top, even_low, odd_top, odd_low):
        return jnp.where(left, even_top, odd_low) + pltpu.roll(
            jnp.where(left, odd_top, even_low), FRAMES, 1)

    def product(a, b, group):
        full = lax.dot_general(a, b, (((0,), (0,)), ((), ())), preferred_element_type=f32)
        for x in range(4):
            top, low = slice(x * 128, x * 128 + 64), slice(x * 128 + 64, x * 128 + 128)
            for e in range(2):
                even, odd = slice(e * 256, e * 256 + 128), slice(e * 256 + 128, e * 256 + 256)
                part = fold(full[top, even], full[low, even], full[top, odd], full[low, odd])
                lanes = slice(group * 256 + e * 128, group * 256 + e * 128 + 128)
                keep_ref[x, :, lanes] = jnp.where(first, part[:32], part[32:])
                send_ref[x * 32:(x + 1) * 32, lanes] = jnp.where(first, part[32:], part[:32])

    def total(b, group):
        full = jnp.dot(ones, b, preferred_element_type=f32)
        for e in range(2):
            even, odd = full[:, e * 256:e * 256 + 128], full[:, e * 256 + 128:e * 256 + 256]
            lanes = slice(group * 256 + e * 128, group * 256 + e * 128 + 128)
            part = fold(even, even, odd, odd)
            own_ref[:, lanes] = part
            send_ref[128:, lanes] = part

    mine, after, prior = matrix(mine_ref), matrix(next_ref), matrix(last_ref)
    product(mine, mine, 1)
    product(mine, prior, 0)
    product(mine, after, 2)
    product(prior, after, 3)
    total(prior, 0)
    total(mine, 1)
    total(after, 2)
    hits = jnp.where(mine_ref[:DEPTH, :].astype(f32) != 0.0, 1.0, 0.0).astype(bf16)
    hits = jnp.dot(ones, hits, preferred_element_type=f32)
    hits = hits + pltpu.roll(hits, FRAMES, 1)
    for e in range(2):
        own_ref[:, 768 + e * 128:896 + e * 128] = hits
        send_ref[128:, 768 + e * 128:896 + e * 128] = hits


def gram(core, mine, after, prior):
    f32 = jnp.float32
    return pl.pallas_call(
        gram_kernel,
        out_shape=(jax.ShapeDtypeStruct((4, 32, 1024), f32),
                   jax.ShapeDtypeStruct((136, 1024), f32),
                   jax.ShapeDtypeStruct((8, 1024), f32)),
        in_specs=[pl.BlockSpec(memory_space=pltpu.SMEM)] + [pl.BlockSpec(memory_space=pltpu.VMEM)] * 3,
        out_specs=(pl.BlockSpec(memory_space=pltpu.VMEM),) * 3,
        compiler_params=pltpu.CompilerParams(vmem_limit_bytes=24 << 20),
        name="gram",
    )(core, mine, after, prior)


def scale_kernel(core_ref, keep_ref, got_ref, own_ref, rows_ref):
    first = core_ref[0] == 0
    sums = own_ref[...] + got_ref[128:, :]
    count = sums[0:1, 768:896]
    count = jnp.concatenate([count, count], axis=1)

    def column(group):
        tall = [jnp.broadcast_to(sums[0:1, group * 256 + e * 128:group * 256 + e * 128 + 128], (128, 128)).T
                for e in range(2)]
        tall = jnp.concatenate(tall, axis=0)
        parts = []
        for x in range(4):
            part = jnp.where(first, tall[x * 64:x * 64 + 32], tall[x * 64 + 32:x * 64 + 64])
            parts.append(jnp.concatenate([part, part], axis=1))
        return parts

    mine, prior = column(1), column(0)
    for x in range(4):
        for group in range(4):
            lanes = slice(group * 256, group * 256 + 256)
            value = keep_ref[x, :, lanes] + got_ref[x * 32:(x + 1) * 32, lanes]
            if group < 3:
                rows_ref[x, :, lanes] = count * value / (mine[x] * sums[0:1, lanes])
            else:
                rows_ref[x, :, lanes] = count * value / (prior[x] * sums[0:1, 512:768])


def scale(core, keep, got, own):
    f32 = jnp.float32
    return pl.pallas_call(
        scale_kernel,
        out_shape=jax.ShapeDtypeStruct((4, 32, 1024), f32),
        in_specs=[pl.BlockSpec(memory_space=pltpu.SMEM)] + [pl.BlockSpec(memory_space=pltpu.VMEM)] * 3,
        out_specs=pl.BlockSpec(memory_space=pltpu.VMEM),
        compiler_params=pltpu.CompilerParams(vmem_limit_bytes=8 << 20),
        name="scale",
    )(core, keep, got, own)


def place_kernel(at_ref, rows_ref, swap_ref, far_ref, cross_ref, out_ref):
    core, row = at_ref[0], at_ref[1]
    own, other = (pl.ds(pl.multiple_of(c * 32, 32), 32) for c in (core, 1 - core))
    for group in range(4):
        lanes = pl.ds(pl.multiple_of(lax.rem(row + 3 + group, 4) * 256, 256), 256)
        source = slice(group * 256, (group + 1) * 256)
        for b in range(2):
            if group < 3:
                out_ref[b, own, lanes] = rows_ref[2 * core + b, :, source]
                out_ref[b, other, lanes] = swap_ref[b, :, source]
            else:
                out_ref[b, own, lanes] = far_ref[b]
                out_ref[b, other, lanes] = cross_ref[b]


def place(at, rows, swap, far, cross):
    return pl.pallas_call(
        place_kernel,
        out_shape=jax.ShapeDtypeStruct((2, 64, 1024), jnp.float32),
        in_specs=[pl.BlockSpec(memory_space=pltpu.SMEM)] + [pl.BlockSpec(memory_space=pltpu.VMEM)] * 4,
        out_specs=pl.BlockSpec(memory_space=pltpu.VMEM),
        compiler_params=pltpu.CompilerParams(vmem_limit_bytes=8 << 20),
        name="place",
    )(at, rows, swap, far, cross)


def shift(size, step):
    return [(i, (i + step) % size) for i in range(size)]


def shards(raw_frames, eigen_flats, weights, flat_count, bin_map):
    core = lax.axis_index("c").astype(jnp.int32)
    row = lax.axis_index("y").astype(jnp.int32)
    packed = pack(weights.T, flat_count[None, :], bin_map.reshape(PIXELS // 128, 128), eigen_flats, raw_frames)
    mine = lax.all_to_all(packed, ("x", "z", "c"), 0, 0, tiled=True).reshape(4 * DEPTH, 128)
    prior = lax.ppermute(mine, "y", shift(4, 1))
    after = lax.ppermute(mine, "y", shift(4, -1))
    keep, send, own = gram(core[None], mine, after, prior)
    got = lax.ppermute(send, "c", shift(2, 1))
    rows = lax.all_to_all(scale(core[None], keep, got, own), "x", 0, 0, tiled=True)
    diagonal = [(c * 4 + y, (1 - c) * 4 + (y + 3) % 4) for c in range(2) for y in range(4)]
    cross = lax.ppermute(lax.dynamic_slice(rows, (2 * (1 - core), 0, 768), (2, 32, 256)), ("c", "y"), diagonal)
    far = lax.ppermute(lax.dynamic_slice(rows, (2 * core, 0, 768), (2, 32, 256)), "y", shift(4, -1))
    swap = lax.ppermute(lax.dynamic_slice(rows, (2 * (1 - core), 0, 0), (2, 32, 768)), "c", shift(2, 1))
    return place(jnp.stack([core, row]), rows, swap, far, cross)


def solution(mesh):
    split = Mesh(mesh.devices.reshape(16, 2, 4, 4), ("z", "c", "y", "x"))
    return jax.shard_map(
        shards,
        mesh=split,
        in_specs=(P(("y", "x"), ("z", "c")), P(None, ("z", "c")), P(("y", "x"), None), P(("y", "x")), P(("z", "c"))),
        out_specs=P(("z", "c"), ("y", "x"), None),
        check_vma=False,
    )
```

```python
import jax, jax.numpy as jnp
from jax import lax
from jax.experimental import pallas as pl
from jax.experimental.pallas import tpu as pltpu
from jax.sharding import Mesh, PartitionSpec as P

CAP = 96
FRAMES = 64
PIXELS = 8192
EIGEN = 16
BINS = 64
CHUNK = 256
CHUNKS = PIXELS // CHUNK
STEP = 512
STEPS = PIXELS // STEP
DEEP = 4
SLOTS = BINS * CAP
PART = 24
DESTS = 128
DEPTH = 32 * PART


def pack_kernel(weights_hbm, used_hbm, bins_hbm, eigen_hbm, raw_hbm, out_ref,
                weights_ref, used_ref, bins_ref, eigen_ref, raw_ref,
                hot_ref, cum_ref, row_ref, place0, place1, place2, place3, even_ref, odd_ref, slot_ref, sems):
    f32, bf16 = jnp.float32, jnp.bfloat16
    sources = (bins_hbm, eigen_hbm, weights_hbm, used_hbm, raw_hbm)
    targets = (bins_ref, eigen_ref, weights_ref, used_ref, raw_ref)
    loads = [pltpu.make_async_copy(a, b, sems.at[i]) for i, (a, b) in enumerate(zip(sources, targets))]
    for load in loads:
        load.start()
    zero = jnp.zeros((128, 128), f32)

    @pl.loop(0, SLOTS // 128)
    def _(i):
        slot_ref[pl.ds(pl.multiple_of(i * 128, 128), 128), :] = zero
    slot_ref[SLOTS:, :] = jnp.zeros((8, 128), f32)
    loads[0].wait()

    label = lax.broadcasted_iota(jnp.int32, (BINS, 128), 0) + 1
    for j in range(CHUNKS):
        for h in range(2):
            hot_ref[j * BINS:(j + 1) * BINS, h * 128:(h + 1) * 128] = jnp.where(
                bins_ref[2 * j + h:2 * j + h + 1, :] == label, 1.0, 0.0).astype(bf16)
    before = lax.broadcasted_iota(jnp.int32, (CHUNK, CHUNK + 128), 0)
    after = lax.broadcasted_iota(jnp.int32, (CHUNK, CHUNK + 128), 1)
    prefix = jnp.where((before < after) | (after >= CHUNK), 1.0, 0.0).astype(bf16)
    cum_ref[...] = jnp.dot(hot_ref[...], prefix, preferred_element_type=f32)
    carry = jnp.zeros((BINS, 128), f32)
    for j in range(CHUNKS):
        rows = slice(j * BINS, (j + 1) * BINS)
        for h in range(2):
            lanes = slice(h * 128, (h + 1) * 128)
            rank = jnp.sum(hot_ref[rows, lanes].astype(f32) * (cum_ref[rows, lanes] + carry), axis=0, keepdims=True)
            own = bins_ref[2 * j + h:2 * j + h + 1, :]
            row_ref[2 * j + h:2 * j + h + 1, :] = jnp.where(
                own > 0, (own - 1) * CAP + rank.astype(jnp.int32), SLOTS)
        carry = carry + cum_ref[rows, CHUNK:]
    places, values = (place0, place1, place2, place3), (even_ref, odd_ref)

    def fetch(j, k):
        rows = pl.ds(pl.multiple_of(j * (STEP // 128), STEP // 128), STEP // 128)
        return pltpu.make_async_copy(row_ref.at[rows, :], places[k], sems.at[5 + k])

    for k in range(DEEP):
        fetch(k, k).start()
    for load in loads[1:]:
        load.wait()

    in_use = lax.broadcasted_iota(jnp.int32, (EIGEN, FRAMES), 0) < used_ref[...]
    coef = jnp.where(in_use, weights_ref[...], 0.0)
    high = coef.astype(bf16)
    rest = coef - high.astype(f32)
    mid = rest.astype(bf16)
    low = (rest - mid.astype(f32)).astype(bf16)
    weights = jnp.concatenate([high.astype(f32), mid.astype(f32), low.astype(f32)], axis=0).T.astype(bf16)

    def correct(j, target):
        at = pl.ds(pl.multiple_of(j * STEP, STEP), STEP)
        flats = eigen_ref[:, at]
        field = 0.5 + jnp.dot(weights, jnp.concatenate([flats] * 3, axis=0), preferred_element_type=f32)
        value = (raw_ref[:, at].astype(f32) / field).astype(bf16).astype(f32)
        for h in range(STEP // 128):
            part = value[:, h * 128:(h + 1) * 128]
            target[h * 128:(h + 1) * 128, :] = jnp.concatenate([part, part], axis=0).T

    def scatter(source, place_ref):
        for i in range(STEP):
            slot_ref[pl.ds(place_ref[i // 128, i % 128], 1), :] = source[i:i + 1, :]

    correct(0, even_ref)

    @pl.loop(0, STEPS // DEEP)
    def _(i):
        for k in range(DEEP):
            fetch(DEEP * i + k, k).wait()
            scatter(values[k % 2], places[k])

            @pl.when(i < STEPS // DEEP - 1)
            def _():
                fetch(DEEP * (i + 1) + k, k).start()
            correct(jnp.minimum(DEEP * i + k + 1, STEPS - 1), values[(k + 1) % 2])

    left = lax.broadcasted_iota(jnp.int32, (PART, 128), 1) < FRAMES

    @pl.loop(0, BINS // 4)
    def _(z):
        for x in range(4):
            for c in range(2):
                base = (4 * z + x) * CAP + c * 2 * PART
                lo = slot_ref[pl.ds(pl.multiple_of(base, 8), PART), :]
                hi = slot_ref[pl.ds(pl.multiple_of(base + PART, 8), PART), :]
                out_ref[x * 32 + 2 * z + c] = jnp.where(left, lo, hi).astype(bf16)


def pack(weights, used, bins, eigen, raw):
    f32 = jnp.float32
    return pl.pallas_call(
        pack_kernel,
        out_shape=jax.ShapeDtypeStruct((DESTS, PART, 128), jnp.bfloat16),
        in_specs=[pl.BlockSpec(memory_space=pltpu.HBM)] * 5,
        out_specs=pl.BlockSpec(memory_space=pltpu.VMEM),
        scratch_shapes=[
            pltpu.VMEM((EIGEN, FRAMES), f32),
            pltpu.VMEM((1, FRAMES), jnp.int32),
            pltpu.VMEM((PIXELS // 128, 128), jnp.int32),
            pltpu.VMEM((EIGEN, PIXELS), jnp.bfloat16),
            pltpu.VMEM((FRAMES, PIXELS), jnp.bfloat16),
            pltpu.VMEM((CHUNKS * BINS, CHUNK), jnp.bfloat16),
            pltpu.VMEM((CHUNKS * BINS, CHUNK + 128), f32),
            pltpu.VMEM((PIXELS // 128, 128), jnp.int32),
            *[pltpu.SMEM((STEP // 128, 128), jnp.int32)] * DEEP,
            pltpu.VMEM((STEP, 128), f32),
            pltpu.VMEM((STEP, 128), f32),
            pltpu.VMEM((SLOTS + 8, 128), f32),
            pltpu.SemaphoreType.DMA((5 + DEEP,)),
        ],
        compiler_params=pltpu.CompilerParams(vmem_limit_bytes=24 << 20),
        name="pack",
    )(*(pltpu.with_memory_space_constraint(a, pltpu.HBM) for a in (weights, used, bins, eigen, raw)))


def gram_kernel(core_ref, mine_ref, next_ref, last_ref, keep_ref, send_ref, own_ref):
    f32, bf16 = jnp.float32, jnp.bfloat16
    first = core_ref[0] == 0
    left = lax.broadcasted_iota(jnp.int32, (1, 128), 1) < FRAMES
    ones = jnp.ones((8, DEPTH), bf16)

    def matrix(ref):
        return jnp.concatenate([ref[x * DEPTH:(x + 1) * DEPTH, :] for x in range(4)], axis=1)

    def fold(even_top, even_low, odd_top, odd_low):
        return jnp.where(left, even_top, odd_low) + pltpu.roll(
            jnp.where(left, odd_top, even_low), FRAMES, 1)

    def product(a, b, group):
        full = lax.dot_general(a, b, (((0,), (0,)), ((), ())), preferred_element_type=f32)
        for x in range(4):
            top, low = slice(x * 128, x * 128 + 64), slice(x * 128 + 64, x * 128 + 128)
            for e in range(2):
                even, odd = slice(e * 256, e * 256 + 128), slice(e * 256 + 128, e * 256 + 256)
                part = fold(full[top, even], full[low, even], full[top, odd], full[low, odd])
                lanes = slice(group * 256 + e * 128, group * 256 + e * 128 + 128)
                keep_ref[x, :, lanes] = jnp.where(first, part[:32], part[32:])
                send_ref[x * 32:(x + 1) * 32, lanes] = jnp.where(first, part[32:], part[:32])

    def total(b, group):
        full = jnp.dot(ones, b, preferred_element_type=f32)
        for e in range(2):
            even, odd = full[:, e * 256:e * 256 + 128], full[:, e * 256 + 128:e * 256 + 256]
            lanes = slice(group * 256 + e * 128, group * 256 + e * 128 + 128)
            part = fold(even, even, odd, odd)
            own_ref[:, lanes] = part
            send_ref[128:, lanes] = part

    mine, after, prior = matrix(mine_ref), matrix(next_ref), matrix(last_ref)
    product(mine, mine, 1)
    product(mine, prior, 0)
    product(mine, after, 2)
    product(prior, after, 3)
    total(prior, 0)
    total(mine, 1)
    total(after, 2)
    hits = jnp.where(mine_ref[:DEPTH, :].astype(f32) != 0.0, 1.0, 0.0).astype(bf16)
    hits = jnp.dot(ones, hits, preferred_element_type=f32)
    hits = hits + pltpu.roll(hits, FRAMES, 1)
    for e in range(2):
        own_ref[:, 768 + e * 128:896 + e * 128] = hits
        send_ref[128:, 768 + e * 128:896 + e * 128] = hits


def gram(core, mine, after, prior):
    f32 = jnp.float32
    return pl.pallas_call(
        gram_kernel,
        out_shape=(jax.ShapeDtypeStruct((4, 32, 1024), f32),
                   jax.ShapeDtypeStruct((136, 1024), f32),
                   jax.ShapeDtypeStruct((8, 1024), f32)),
        in_specs=[pl.BlockSpec(memory_space=pltpu.SMEM)] + [pl.BlockSpec(memory_space=pltpu.VMEM)] * 3,
        out_specs=(pl.BlockSpec(memory_space=pltpu.VMEM),) * 3,
        compiler_params=pltpu.CompilerParams(vmem_limit_bytes=24 << 20),
        name="gram",
    )(core, mine, after, prior)


def scale_kernel(core_ref, keep_ref, got_ref, own_ref, rows_ref):
    first = core_ref[0] == 0
    sums = own_ref[...] + got_ref[128:, :]
    count = sums[0:1, 768:896]
    count = jnp.concatenate([count, count], axis=1)

    def column(group):
        tall = [jnp.broadcast_to(sums[0:1, group * 256 + e * 128:group * 256 + e * 128 + 128], (128, 128)).T
                for e in range(2)]
        tall = jnp.concatenate(tall, axis=0)
        parts = []
        for x in range(4):
            part = jnp.where(first, tall[x * 64:x * 64 + 32], tall[x * 64 + 32:x * 64 + 64])
            parts.append(jnp.concatenate([part, part], axis=1))
        return parts

    mine, prior = column(1), column(0)
    for x in range(4):
        for group in range(4):
            lanes = slice(group * 256, group * 256 + 256)
            value = keep_ref[x, :, lanes] + got_ref[x * 32:(x + 1) * 32, lanes]
            if group < 3:
                rows_ref[x, :, lanes] = count * value / (mine[x] * sums[0:1, lanes])
            else:
                rows_ref[x, :, lanes] = count * value / (prior[x] * sums[0:1, 512:768])


def scale(core, keep, got, own):
    f32 = jnp.float32
    return pl.pallas_call(
        scale_kernel,
        out_shape=jax.ShapeDtypeStruct((4, 32, 1024), f32),
        in_specs=[pl.BlockSpec(memory_space=pltpu.SMEM)] + [pl.BlockSpec(memory_space=pltpu.VMEM)] * 3,
        out_specs=pl.BlockSpec(memory_space=pltpu.VMEM),
        compiler_params=pltpu.CompilerParams(vmem_limit_bytes=8 << 20),
        name="scale",
    )(core, keep, got, own)


def place_kernel(at_ref, rows_ref, swap_ref, far_ref, cross_ref, out_ref):
    core, row = at_ref[0], at_ref[1]
    own, other = (pl.ds(pl.multiple_of(c * 32, 32), 32) for c in (core, 1 - core))
    for group in range(4):
        lanes = pl.ds(pl.multiple_of(lax.rem(row + 3 + group, 4) * 256, 256), 256)
        source = slice(group * 256, (group + 1) * 256)
        for b in range(2):
            if group < 3:
                out_ref[b, own, lanes] = rows_ref[2 * core + b, :, source]
                out_ref[b, other, lanes] = swap_ref[b, :, source]
            else:
                out_ref[b, own, lanes] = far_ref[b]
                out_ref[b, other, lanes] = cross_ref[b]


def place(at, rows, swap, far, cross):
    return pl.pallas_call(
        place_kernel,
        out_shape=jax.ShapeDtypeStruct((2, 64, 1024), jnp.float32),
        in_specs=[pl.BlockSpec(memory_space=pltpu.SMEM)] + [pl.BlockSpec(memory_space=pltpu.VMEM)] * 4,
        out_specs=pl.BlockSpec(memory_space=pltpu.VMEM),
        compiler_params=pltpu.CompilerParams(vmem_limit_bytes=8 << 20),
        name="place",
    )(at, rows, swap, far, cross)


def shift(size, step):
    return [(i, (i + step) % size) for i in range(size)]


def shards(raw_frames, eigen_flats, weights, flat_count, bin_map):
    core = lax.axis_index("c").astype(jnp.int32)
    row = lax.axis_index("y").astype(jnp.int32)
    packed = pack(weights.T, flat_count[None, :], bin_map.reshape(PIXELS // 128, 128), eigen_flats, raw_frames)
    mine = lax.all_to_all(packed, ("x", "z", "c"), 0, 0, tiled=True).reshape(4 * DEPTH, 128)
    prior = lax.ppermute(mine, "y", shift(4, 1))
    after = lax.ppermute(mine, "y", shift(4, -1))
    keep, send, own = gram(core[None], mine, after, prior)
    got = lax.ppermute(send, "c", shift(2, 1))
    rows = lax.all_to_all(scale(core[None], keep, got, own), "x", 0, 0, tiled=True)
    diagonal = [(c * 4 + y, (1 - c) * 4 + (y + 3) % 4) for c in range(2) for y in range(4)]
    cross = lax.ppermute(lax.dynamic_slice(rows, (2 * (1 - core), 0, 768), (2, 32, 256)), ("c", "y"), diagonal)
    far = lax.ppermute(lax.dynamic_slice(rows, (2 * core, 0, 768), (2, 32, 256)), "y", shift(4, -1))
    swap = lax.ppermute(lax.dynamic_slice(rows, (2 * (1 - core), 0, 0), (2, 32, 768)), "c", shift(2, 1))
    return place(jnp.stack([core, row]), rows, swap, far, cross)


def solution(mesh):
    split = Mesh(mesh.devices.reshape(16, 2, 4, 4), ("z", "c", "y", "x"))
    return jax.shard_map(
        shards,
        mesh=split,
        in_specs=(P(("y", "x"), ("z", "c")), P(None, ("z", "c")), P(("y", "x"), None), P(("y", "x")), P(("z", "c"))),
        out_specs=P(("z", "c"), ("y", "x"), None),
        check_vma=False,
    )
```

```python
import jax, jax.numpy as jnp
from jax import lax
from jax.experimental import pallas as pl
from jax.experimental.pallas import tpu as pltpu
from jax.sharding import Mesh, PartitionSpec as P

CAP = 96
FRAMES = 64
PIXELS = 8192
EIGEN = 16
BINS = 64
CHUNK = 256
CHUNKS = PIXELS // CHUNK
STEP = 512
STEPS = PIXELS // STEP
DEEP = 4
SLOTS = BINS * CAP
PART = CAP // 2
DESTS = 64
DEPTH = 16 * PART


def pack_kernel(weights_hbm, used_hbm, bins_hbm, eigen_hbm, raw_hbm, out_ref,
                weights_ref, used_ref, bins_ref, eigen_ref, raw_ref,
                hot_ref, cum_ref, row_ref, place0, place1, place2, place3, even_ref, odd_ref, slot_ref, sems):
    f32, bf16 = jnp.float32, jnp.bfloat16
    sources = (bins_hbm, eigen_hbm, weights_hbm, used_hbm, raw_hbm)
    targets = (bins_ref, eigen_ref, weights_ref, used_ref, raw_ref)
    loads = [pltpu.make_async_copy(a, b, sems.at[i]) for i, (a, b) in enumerate(zip(sources, targets))]
    for load in loads:
        load.start()
    zero = jnp.zeros((128, 128), f32)

    @pl.loop(0, SLOTS // 128)
    def _(i):
        slot_ref[pl.ds(pl.multiple_of(i * 128, 128), 128), :] = zero
    slot_ref[SLOTS:, :] = jnp.zeros((8, 128), f32)
    loads[0].wait()

    label = lax.broadcasted_iota(jnp.int32, (BINS, 128), 0) + 1
    for j in range(CHUNKS):
        for h in range(2):
            hot_ref[j * BINS:(j + 1) * BINS, h * 128:(h + 1) * 128] = jnp.where(
                bins_ref[2 * j + h:2 * j + h + 1, :] == label, 1.0, 0.0).astype(bf16)
    before = lax.broadcasted_iota(jnp.int32, (CHUNK, CHUNK + 128), 0)
    after = lax.broadcasted_iota(jnp.int32, (CHUNK, CHUNK + 128), 1)
    prefix = jnp.where((before < after) | (after >= CHUNK), 1.0, 0.0).astype(bf16)
    cum_ref[...] = jnp.dot(hot_ref[...], prefix, preferred_element_type=f32)
    carry = jnp.zeros((BINS, 128), f32)
    for j in range(CHUNKS):
        rows = slice(j * BINS, (j + 1) * BINS)
        for h in range(2):
            lanes = slice(h * 128, (h + 1) * 128)
            rank = jnp.sum(hot_ref[rows, lanes].astype(f32) * (cum_ref[rows, lanes] + carry), axis=0, keepdims=True)
            own = bins_ref[2 * j + h:2 * j + h + 1, :]
            row_ref[2 * j + h:2 * j + h + 1, :] = jnp.where(
                own > 0, (own - 1) * CAP + rank.astype(jnp.int32), SLOTS)
        carry = carry + cum_ref[rows, CHUNK:]
    places, values = (place0, place1, place2, place3), (even_ref, odd_ref)

    def fetch(j, k):
        rows = pl.ds(pl.multiple_of(j * (STEP // 128), STEP // 128), STEP // 128)
        return pltpu.make_async_copy(row_ref.at[rows, :], places[k], sems.at[5 + k])

    for k in range(DEEP):
        fetch(k, k).start()
    for load in loads[1:]:
        load.wait()

    in_use = lax.broadcasted_iota(jnp.int32, (EIGEN, FRAMES), 0) < used_ref[...]
    coef = jnp.where(in_use, weights_ref[...], 0.0)
    high = coef.astype(bf16)
    rest = coef - high.astype(f32)
    mid = rest.astype(bf16)
    low = (rest - mid.astype(f32)).astype(bf16)
    weights = jnp.concatenate([high.astype(f32), mid.astype(f32), low.astype(f32)], axis=0).T.astype(bf16)

    def correct(j, target):
        at = pl.ds(pl.multiple_of(j * STEP, STEP), STEP)
        flats = eigen_ref[:, at]
        field = 0.5 + jnp.dot(weights, jnp.concatenate([flats] * 3, axis=0), preferred_element_type=f32)
        value = (raw_ref[:, at].astype(f32) / field).astype(bf16).astype(f32)
        for h in range(STEP // 128):
            part = value[:, h * 128:(h + 1) * 128]
            target[h * 128:(h + 1) * 128, :] = jnp.concatenate([part, part], axis=0).T

    def scatter(source, place_ref):
        for i in range(STEP):
            slot_ref[pl.ds(place_ref[i // 128, i % 128], 1), :] = source[i:i + 1, :]

    correct(0, even_ref)

    @pl.loop(0, STEPS // DEEP)
    def _(i):
        for k in range(DEEP):
            fetch(DEEP * i + k, k).wait()
            scatter(values[k % 2], places[k])

            @pl.when(i < STEPS // DEEP - 1)
            def _():
                fetch(DEEP * (i + 1) + k, k).start()
            correct(jnp.minimum(DEEP * i + k + 1, STEPS - 1), values[(k + 1) % 2])

    left = lax.broadcasted_iota(jnp.int32, (PART, 128), 1) < FRAMES

    @pl.loop(0, BINS // 4)
    def _(z):
        for x in range(4):
            base = (4 * z + x) * CAP
            lo = slot_ref[pl.ds(pl.multiple_of(base, 8), PART), :]
            hi = slot_ref[pl.ds(pl.multiple_of(base + PART, 8), PART), :]
            out_ref[x * 16 + z] = jnp.where(left, lo, hi).astype(bf16)


def pack(weights, used, bins, eigen, raw):
    f32 = jnp.float32
    return pl.pallas_call(
        pack_kernel,
        out_shape=jax.ShapeDtypeStruct((DESTS, PART, 128), jnp.bfloat16),
        in_specs=[pl.BlockSpec(memory_space=pltpu.HBM)] * 5,
        out_specs=pl.BlockSpec(memory_space=pltpu.VMEM),
        scratch_shapes=[
            pltpu.VMEM((EIGEN, FRAMES), f32),
            pltpu.VMEM((1, FRAMES), jnp.int32),
            pltpu.VMEM((PIXELS // 128, 128), jnp.int32),
            pltpu.VMEM((EIGEN, PIXELS), jnp.bfloat16),
            pltpu.VMEM((FRAMES, PIXELS), jnp.bfloat16),
            pltpu.VMEM((CHUNKS * BINS, CHUNK), jnp.bfloat16),
            pltpu.VMEM((CHUNKS * BINS, CHUNK + 128), f32),
            pltpu.VMEM((PIXELS // 128, 128), jnp.int32),
            *[pltpu.SMEM((STEP // 128, 128), jnp.int32)] * DEEP,
            pltpu.VMEM((STEP, 128), f32),
            pltpu.VMEM((STEP, 128), f32),
            pltpu.VMEM((SLOTS + 8, 128), f32),
            pltpu.SemaphoreType.DMA((5 + DEEP,)),
        ],
        compiler_params=pltpu.CompilerParams(vmem_limit_bytes=24 << 20),
        name="pack",
    )(*(pltpu.with_memory_space_constraint(a, pltpu.HBM) for a in (weights, used, bins, eigen, raw)))


def gram_kernel(core_ref, mine_ref, next_ref, last_ref, keep_ref, send_ref, own_ref):
    f32, bf16 = jnp.float32, jnp.bfloat16
    first = core_ref[0] == 0
    left = lax.broadcasted_iota(jnp.int32, (1, 128), 1) < FRAMES
    ones = jnp.ones((8, DEPTH), bf16)

    def matrix(ref):
        return jnp.concatenate([ref[x * DEPTH:(x + 1) * DEPTH, :] for x in range(4)], axis=1)

    def fold(even_top, even_low, odd_top, odd_low):
        return jnp.where(left, even_top, odd_low) + pltpu.roll(
            jnp.where(left, odd_top, even_low), FRAMES, 1)

    def product(a, b, group):
        full = lax.dot_general(a, b, (((0,), (0,)), ((), ())), preferred_element_type=f32)
        for x in range(4):
            top, low = slice(x * 128, x * 128 + 64), slice(x * 128 + 64, x * 128 + 128)
            for e in range(2):
                even, odd = slice(e * 256, e * 256 + 128), slice(e * 256 + 128, e * 256 + 256)
                part = fold(full[top, even], full[low, even], full[top, odd], full[low, odd])
                lanes = slice(group * 256 + e * 128, group * 256 + e * 128 + 128)
                keep_ref[x, :, lanes] = jnp.where(first, part[:32], part[32:])
                send_ref[x * 32:(x + 1) * 32, lanes] = jnp.where(first, part[32:], part[:32])

    def total(b, group):
        full = jnp.dot(ones, b, preferred_element_type=f32)
        for e in range(2):
            even, odd = full[:, e * 256:e * 256 + 128], full[:, e * 256 + 128:e * 256 + 256]
            lanes = slice(group * 256 + e * 128, group * 256 + e * 128 + 128)
            part = fold(even, even, odd, odd)
            own_ref[:, lanes] = part
            send_ref[128:, lanes] = part

    mine, after, prior = matrix(mine_ref), matrix(next_ref), matrix(last_ref)
    product(mine, mine, 1)
    product(mine, prior, 0)
    product(mine, after, 2)
    product(prior, after, 3)
    total(prior, 0)
    total(mine, 1)
    total(after, 2)
    hits = jnp.where(mine_ref[:DEPTH, :].astype(f32) != 0.0, 1.0, 0.0).astype(bf16)
    hits = jnp.dot(ones, hits, preferred_element_type=f32)
    hits = hits + pltpu.roll(hits, FRAMES, 1)
    for e in range(2):
        own_ref[:, 768 + e * 128:896 + e * 128] = hits
        send_ref[128:, 768 + e * 128:896 + e * 128] = hits


def gram(core, mine, after, prior):
    f32 = jnp.float32
    return pl.pallas_call(
        gram_kernel,
        out_shape=(jax.ShapeDtypeStruct((4, 32, 1024), f32),
                   jax.ShapeDtypeStruct((136, 1024), f32),
                   jax.ShapeDtypeStruct((8, 1024), f32)),
        in_specs=[pl.BlockSpec(memory_space=pltpu.SMEM)] + [pl.BlockSpec(memory_space=pltpu.VMEM)] * 3,
        out_specs=(pl.BlockSpec(memory_space=pltpu.VMEM),) * 3,
        compiler_params=pltpu.CompilerParams(vmem_limit_bytes=24 << 20),
        name="gram",
    )(core, mine, after, prior)


def scale_kernel(core_ref, keep_ref, got_ref, own_ref, rows_ref):
    first = core_ref[0] == 0
    sums = own_ref[...] + got_ref[128:, :]
    count = sums[0:1, 768:896]
    count = jnp.concatenate([count, count], axis=1)

    def column(group):
        tall = [jnp.broadcast_to(sums[0:1, group * 256 + e * 128:group * 256 + e * 128 + 128], (128, 128)).T
                for e in range(2)]
        tall = jnp.concatenate(tall, axis=0)
        parts = []
        for x in range(4):
            part = jnp.where(first, tall[x * 64:x * 64 + 32], tall[x * 64 + 32:x * 64 + 64])
            parts.append(jnp.concatenate([part, part], axis=1))
        return parts

    mine, prior = column(1), column(0)
    for x in range(4):
        for group in range(4):
            lanes = slice(group * 256, group * 256 + 256)
            value = keep_ref[x, :, lanes] + got_ref[x * 32:(x + 1) * 32, lanes]
            if group < 3:
                rows_ref[x, :, lanes] = count * value / (mine[x] * sums[0:1, lanes])
            else:
                rows_ref[x, :, lanes] = count * value / (prior[x] * sums[0:1, 512:768])


def scale(core, keep, got, own):
    f32 = jnp.float32
    return pl.pallas_call(
        scale_kernel,
        out_shape=jax.ShapeDtypeStruct((4, 32, 1024), f32),
        in_specs=[pl.BlockSpec(memory_space=pltpu.SMEM)] + [pl.BlockSpec(memory_space=pltpu.VMEM)] * 3,
        out_specs=pl.BlockSpec(memory_space=pltpu.VMEM),
        compiler_params=pltpu.CompilerParams(vmem_limit_bytes=8 << 20),
        name="scale",
    )(core, keep, got, own)


def place_kernel(at_ref, rows_ref, swap_ref, far_ref, out_ref):
    core, row = at_ref[0], at_ref[1]
    own, other = (pl.ds(pl.multiple_of(c * 32, 32), 32) for c in (core, 1 - core))
    for group in range(4):
        lanes = pl.ds(pl.multiple_of(lax.rem(row + 3 + group, 4) * 256, 256), 256)
        source = slice(group * 256, (group + 1) * 256)
        for b in range(2):
            if group < 3:
                out_ref[b, own, lanes] = rows_ref[2 * core + b, :, source]
                out_ref[b, other, lanes] = swap_ref[b, :, source]
            else:
                out_ref[b, own, lanes] = far_ref[b]
                out_ref[b, other, lanes] = far_ref[2 + b]


def place(at, rows, swap, far):
    return pl.pallas_call(
        place_kernel,
        out_shape=jax.ShapeDtypeStruct((2, 64, 1024), jnp.float32),
        in_specs=[pl.BlockSpec(memory_space=pltpu.SMEM)] + [pl.BlockSpec(memory_space=pltpu.VMEM)] * 3,
        out_specs=pl.BlockSpec(memory_space=pltpu.VMEM),
        compiler_params=pltpu.CompilerParams(vmem_limit_bytes=8 << 20),
        name="place",
    )(at, rows, swap, far)


def shift(size, step):
    return [(i, (i + step) % size) for i in range(size)]


def shards(raw_frames, eigen_flats, weights, flat_count, bin_map):
    core = lax.axis_index("c").astype(jnp.int32)
    row = lax.axis_index("y").astype(jnp.int32)
    packed = pack(weights.T, flat_count[None, :], bin_map.reshape(PIXELS // 128, 128), eigen_flats, raw_frames)
    mine = lax.all_to_all(packed, ("x", "z"), 0, 0, tiled=True).reshape(4 * DEPTH, 128)
    prior = lax.ppermute(mine, "y", shift(4, 1))
    after = lax.ppermute(mine, "y", shift(4, -1))
    keep, send, own = gram(core[None], mine, after, prior)
    got = lax.ppermute(send, "c", shift(2, 1))
    rows = lax.all_to_all(scale(core[None], keep, got, own), "x", 0, 0, tiled=True)
    swap = lax.ppermute(lax.dynamic_slice_in_dim(rows, 2 * (1 - core), 2, 0), "c", shift(2, 1))
    far = jnp.concatenate([lax.dynamic_slice(rows, (2 * core, 0, 768), (2, 32, 256)), swap[:, :, 768:]], axis=0)
    far = lax.ppermute(far, "y", shift(4, -1))
    return place(jnp.stack([core, row]), rows, swap, far)


def solution(mesh):
    split = Mesh(mesh.devices.reshape(16, 2, 4, 4), ("z", "c", "y", "x"))
    return jax.shard_map(
        shards,
        mesh=split,
        in_specs=(P(("y", "x"), ("z", "c")), P(None, ("z", "c")), P(("y", "x"), None), P(("y", "x")), P(("z", "c"))),
        out_specs=P(("z", "c"), ("y", "x"), None),
        check_vma=False,
    )
```

```python
import jax, jax.numpy as jnp
from jax import lax
from jax.experimental import pallas as pl
from jax.experimental.pallas import tpu as pltpu
from jax.sharding import Mesh, PartitionSpec as P

CAP = 96
FRAMES = 64
PIXELS = 8192
EIGEN = 16
BINS = 64
CHUNK = 256
CHUNKS = PIXELS // CHUNK
STEP = 512
STEPS = PIXELS // STEP
DEEP = 4
SLOTS = BINS * CAP
PART = CAP // 2
DESTS = 64
DEPTH = 16 * PART


def pack_kernel(weights_hbm, used_hbm, bins_hbm, eigen_hbm, raw_hbm, out_ref,
                weights_ref, used_ref, bins_ref, eigen_ref, raw_ref,
                hot_ref, cum_ref, row_ref, place0, place1, place2, place3, even_ref, odd_ref, slot_ref, sems):
    f32, bf16 = jnp.float32, jnp.bfloat16
    sources = (bins_hbm, eigen_hbm, weights_hbm, used_hbm, raw_hbm)
    targets = (bins_ref, eigen_ref, weights_ref, used_ref, raw_ref)
    loads = [pltpu.make_async_copy(a, b, sems.at[i]) for i, (a, b) in enumerate(zip(sources, targets))]
    for load in loads:
        load.start()
    zero = jnp.zeros((128, 128), f32)

    @pl.loop(0, SLOTS // 128)
    def _(i):
        slot_ref[pl.ds(pl.multiple_of(i * 128, 128), 128), :] = zero
    slot_ref[SLOTS:, :] = jnp.zeros((8, 128), f32)
    loads[0].wait()

    label = lax.broadcasted_iota(jnp.int32, (BINS, 128), 0) + 1
    for j in range(CHUNKS):
        for h in range(2):
            hot_ref[j * BINS:(j + 1) * BINS, h * 128:(h + 1) * 128] = jnp.where(
                bins_ref[2 * j + h:2 * j + h + 1, :] == label, 1.0, 0.0).astype(bf16)
    before = lax.broadcasted_iota(jnp.int32, (CHUNK, CHUNK + 128), 0)
    after = lax.broadcasted_iota(jnp.int32, (CHUNK, CHUNK + 128), 1)
    prefix = jnp.where((before < after) | (after >= CHUNK), 1.0, 0.0).astype(bf16)
    cum_ref[...] = jnp.dot(hot_ref[...], prefix, preferred_element_type=f32)
    carry = jnp.zeros((BINS, 128), f32)
    for j in range(CHUNKS):
        rows = slice(j * BINS, (j + 1) * BINS)
        for h in range(2):
            lanes = slice(h * 128, (h + 1) * 128)
            rank = jnp.sum(hot_ref[rows, lanes].astype(f32) * (cum_ref[rows, lanes] + carry), axis=0, keepdims=True)
            own = bins_ref[2 * j + h:2 * j + h + 1, :]
            row_ref[2 * j + h:2 * j + h + 1, :] = jnp.where(
                own > 0, (own - 1) * CAP + rank.astype(jnp.int32), SLOTS)
        carry = carry + cum_ref[rows, CHUNK:]
    places, values = (place0, place1, place2, place3), (even_ref, odd_ref)

    def fetch(j, k):
        rows = pl.ds(pl.multiple_of(j * (STEP // 128), STEP // 128), STEP // 128)
        return pltpu.make_async_copy(row_ref.at[rows, :], places[k], sems.at[5 + k])

    for k in range(DEEP):
        fetch(k, k).start()
    for load in loads[1:]:
        load.wait()

    in_use = lax.broadcasted_iota(jnp.int32, (EIGEN, FRAMES), 0) < used_ref[...]
    coef = jnp.where(in_use, weights_ref[...], 0.0)
    high = coef.astype(bf16)
    rest = coef - high.astype(f32)
    mid = rest.astype(bf16)
    low = (rest - mid.astype(f32)).astype(bf16)
    weights = jnp.concatenate([high.astype(f32), mid.astype(f32), low.astype(f32)], axis=0).T.astype(bf16)

    def correct(j, target):
        at = pl.ds(pl.multiple_of(j * STEP, STEP), STEP)
        flats = eigen_ref[:, at]
        field = 0.5 + jnp.dot(weights, jnp.concatenate([flats] * 3, axis=0), preferred_element_type=f32)
        value = (raw_ref[:, at].astype(f32) / field).astype(bf16).astype(f32)
        for h in range(STEP // 128):
            part = value[:, h * 128:(h + 1) * 128]
            target[h * 128:(h + 1) * 128, :] = jnp.concatenate([part, part], axis=0).T

    def scatter(source, place_ref):
        for i in range(STEP):
            slot_ref[pl.ds(place_ref[i // 128, i % 128], 1), :] = source[i:i + 1, :]

    correct(0, even_ref)

    @pl.loop(0, STEPS // DEEP)
    def _(i):
        for k in range(DEEP):
            fetch(DEEP * i + k, k).wait()
            scatter(values[k % 2], places[k])

            @pl.when(i < STEPS // DEEP - 1)
            def _():
                fetch(DEEP * (i + 1) + k, k).start()
            correct(jnp.minimum(DEEP * i + k + 1, STEPS - 1), values[(k + 1) % 2])

    left = lax.broadcasted_iota(jnp.int32, (PART, 128), 1) < FRAMES

    @pl.loop(0, BINS // 4)
    def _(z):
        for x in range(4):
            base = (4 * z + x) * CAP
            lo = slot_ref[pl.ds(pl.multiple_of(base, 8), PART), :]
            hi = slot_ref[pl.ds(pl.multiple_of(base + PART, 8), PART), :]
            out_ref[x * 16 + z] = jnp.where(left, lo, hi).astype(bf16)


def pack(weights, used, bins, eigen, raw):
    f32 = jnp.float32
    return pl.pallas_call(
        pack_kernel,
        out_shape=jax.ShapeDtypeStruct((DESTS, PART, 128), jnp.bfloat16),
        in_specs=[pl.BlockSpec(memory_space=pltpu.HBM)] * 5,
        out_specs=pl.BlockSpec(memory_space=pltpu.VMEM),
        scratch_shapes=[
            pltpu.VMEM((EIGEN, FRAMES), f32),
            pltpu.VMEM((1, FRAMES), jnp.int32),
            pltpu.VMEM((PIXELS // 128, 128), jnp.int32),
            pltpu.VMEM((EIGEN, PIXELS), jnp.bfloat16),
            pltpu.VMEM((FRAMES, PIXELS), jnp.bfloat16),
            pltpu.VMEM((CHUNKS * BINS, CHUNK), jnp.bfloat16),
            pltpu.VMEM((CHUNKS * BINS, CHUNK + 128), f32),
            pltpu.VMEM((PIXELS // 128, 128), jnp.int32),
            *[pltpu.SMEM((STEP // 128, 128), jnp.int32)] * DEEP,
            pltpu.VMEM((STEP, 128), f32),
            pltpu.VMEM((STEP, 128), f32),
            pltpu.VMEM((SLOTS + 8, 128), f32),
            pltpu.SemaphoreType.DMA((5 + DEEP,)),
        ],
        compiler_params=pltpu.CompilerParams(vmem_limit_bytes=24 << 20),
        name="pack",
    )(*(pltpu.with_memory_space_constraint(a, pltpu.HBM) for a in (weights, used, bins, eigen, raw)))


def gram_kernel(core_ref, mine_ref, next_ref, last_ref, keep_ref, send_ref, own_ref):
    f32, bf16 = jnp.float32, jnp.bfloat16
    first = core_ref[0] == 0
    left = lax.broadcasted_iota(jnp.int32, (1, 128), 1) < FRAMES
    ones = jnp.ones((8, DEPTH), bf16)

    def matrix(ref):
        return jnp.concatenate([ref[x * DEPTH:(x + 1) * DEPTH, :] for x in range(4)], axis=1)

    def fold(even_top, even_low, odd_top, odd_low):
        return jnp.where(left, even_top, odd_low) + pltpu.roll(
            jnp.where(left, odd_top, even_low), FRAMES, 1)

    def product(a, b, group):
        full = lax.dot_general(a, b, (((0,), (0,)), ((), ())), preferred_element_type=f32)
        for x in range(4):
            top, low = slice(x * 128, x * 128 + 64), slice(x * 128 + 64, x * 128 + 128)
            for e in range(2):
                even, odd = slice(e * 256, e * 256 + 128), slice(e * 256 + 128, e * 256 + 256)
                part = fold(full[top, even], full[low, even], full[top, odd], full[low, odd])
                lanes = slice(group * 256 + e * 128, group * 256 + e * 128 + 128)
                keep_ref[x, :, lanes] = jnp.where(first, part[:32], part[32:])
                send_ref[x * 32:(x + 1) * 32, lanes] = jnp.where(first, part[32:], part[:32])

    def total(b, group):
        full = jnp.dot(ones, b, preferred_element_type=f32)
        for e in range(2):
            even, odd = full[:, e * 256:e * 256 + 128], full[:, e * 256 + 128:e * 256 + 256]
            lanes = slice(group * 256 + e * 128, group * 256 + e * 128 + 128)
            part = fold(even, even, odd, odd)
            own_ref[:, lanes] = part
            send_ref[128:, lanes] = part

    mine, after, prior = matrix(mine_ref), matrix(next_ref), matrix(last_ref)
    product(mine, mine, 1)
    product(mine, prior, 0)
    product(mine, after, 2)
    product(prior, after, 3)
    total(prior, 0)
    total(mine, 1)
    total(after, 2)
    hits = jnp.where(mine_ref[:DEPTH, :].astype(f32) != 0.0, 1.0, 0.0).astype(bf16)
    hits = jnp.dot(ones, hits, preferred_element_type=f32)
    hits = hits + pltpu.roll(hits, FRAMES, 1)
    for e in range(2):
        own_ref[:, 768 + e * 128:896 + e * 128] = hits
        send_ref[128:, 768 + e * 128:896 + e * 128] = hits


def gram(core, mine, after, prior):
    f32 = jnp.float32
    return pl.pallas_call(
        gram_kernel,
        out_shape=(jax.ShapeDtypeStruct((4, 32, 1024), f32),
                   jax.ShapeDtypeStruct((136, 1024), f32),
                   jax.ShapeDtypeStruct((8, 1024), f32)),
        in_specs=[pl.BlockSpec(memory_space=pltpu.SMEM)] + [pl.BlockSpec(memory_space=pltpu.VMEM)] * 3,
        out_specs=(pl.BlockSpec(memory_space=pltpu.VMEM),) * 3,
        compiler_params=pltpu.CompilerParams(vmem_limit_bytes=24 << 20),
        name="gram",
    )(core, mine, after, prior)


def scale_kernel(core_ref, keep_ref, got_ref, own_ref, rows_ref):
    first = core_ref[0] == 0
    sums = own_ref[...] + got_ref[128:, :]
    count = sums[0:1, 768:896]
    count = jnp.concatenate([count, count], axis=1)

    def column(group):
        tall = [jnp.broadcast_to(sums[0:1, group * 256 + e * 128:group * 256 + e * 128 + 128], (128, 128)).T
                for e in range(2)]
        tall = jnp.concatenate(tall, axis=0)
        parts = []
        for x in range(4):
            part = jnp.where(first, tall[x * 64:x * 64 + 32], tall[x * 64 + 32:x * 64 + 64])
            parts.append(jnp.concatenate([part, part], axis=1))
        return parts

    mine, prior = column(1), column(0)
    for x in range(4):
        for group in range(4):
            lanes = slice(group * 256, group * 256 + 256)
            value = keep_ref[x, :, lanes] + got_ref[x * 32:(x + 1) * 32, lanes]
            if group < 3:
                rows_ref[x, :, lanes] = count * value / (mine[x] * sums[0:1, lanes])
            else:
                rows_ref[x, :, lanes] = count * value / (prior[x] * sums[0:1, 512:768])


def scale(core, keep, got, own):
    f32 = jnp.float32
    return pl.pallas_call(
        scale_kernel,
        out_shape=jax.ShapeDtypeStruct((4, 32, 1024), f32),
        in_specs=[pl.BlockSpec(memory_space=pltpu.SMEM)] + [pl.BlockSpec(memory_space=pltpu.VMEM)] * 3,
        out_specs=pl.BlockSpec(memory_space=pltpu.VMEM),
        compiler_params=pltpu.CompilerParams(vmem_limit_bytes=8 << 20),
        name="scale",
    )(core, keep, got, own)


def place_kernel(at_ref, rows_ref, swap_ref, far_ref, out_ref):
    core, row = at_ref[0], at_ref[1]
    own, other = (pl.ds(pl.multiple_of(c * 32, 32), 32) for c in (core, 1 - core))
    for group in range(4):
        lanes = pl.ds(pl.multiple_of(lax.rem(row + 3 + group, 4) * 256, 256), 256)
        source = slice(group * 256, (group + 1) * 256)
        for b in range(2):
            if group < 3:
                out_ref[b, own, lanes] = rows_ref[2 * core + b, :, source]
                out_ref[b, other, lanes] = swap_ref[b, :, source]
            else:
                out_ref[b, own, lanes] = far_ref[b]
                out_ref[b, other, lanes] = far_ref[2 + b]


def place(at, rows, swap, far):
    return pl.pallas_call(
        place_kernel,
        out_shape=jax.ShapeDtypeStruct((2, 64, 1024), jnp.float32),
        in_specs=[pl.BlockSpec(memory_space=pltpu.SMEM)] + [pl.BlockSpec(memory_space=pltpu.VMEM)] * 3,
        out_specs=pl.BlockSpec(memory_space=pltpu.VMEM),
        compiler_params=pltpu.CompilerParams(vmem_limit_bytes=8 << 20),
        name="place",
    )(at, rows, swap, far)


def shift(size, step):
    return [(i, (i + step) % size) for i in range(size)]


def shards(raw_frames, eigen_flats, weights, flat_count, bin_map):
    core = lax.axis_index("c").astype(jnp.int32)
    row = lax.axis_index("y").astype(jnp.int32)
    packed = pack(weights.T, flat_count[None, :], bin_map.reshape(PIXELS // 128, 128), eigen_flats, raw_frames)
    mine = lax.all_to_all(packed, ("x", "z"), 0, 0, tiled=True).reshape(4 * DEPTH, 128)
    prior = lax.ppermute(mine, "y", shift(4, 1))
    after = lax.ppermute(mine, "y", shift(4, -1))
    keep, send, own = gram(core[None], mine, after, prior)
    got = lax.ppermute(send, "c", shift(2, 1))
    first, second, at, rows = lax.optimization_barrier(
        (2 * core, 2 - 2 * core, jnp.stack([core, row]), scale(core[None], keep, got, own)))
    rows = lax.all_to_all(rows, "x", 0, 0, tiled=True)
    swap = lax.ppermute(lax.dynamic_slice_in_dim(rows, second, 2, 0, allow_negative_indices=False), "c", shift(2, 1))
    far = jnp.concatenate([lax.dynamic_slice(rows, (first, 0, 768), (2, 32, 256), allow_negative_indices=False), swap[:, :, 768:]], axis=0)
    far = lax.ppermute(far, "y", shift(4, -1))
    return place(at, rows, swap, far)


def solution(mesh):
    split = Mesh(mesh.devices.reshape(16, 2, 4, 4), ("z", "c", "y", "x"))
    return jax.shard_map(
        shards,
        mesh=split,
        in_specs=(P(("y", "x"), ("z", "c")), P(None, ("z", "c")), P(("y", "x"), None), P(("y", "x")), P(("z", "c"))),
        out_specs=P(("z", "c"), ("y", "x"), None),
        check_vma=False,
    )
```

```python
import jax, jax.numpy as jnp
from jax import lax
from jax.experimental import pallas as pl
from jax.experimental.pallas import tpu as pltpu
from jax.sharding import Mesh, PartitionSpec as P

CAP = 96
FRAMES = 64
PIXELS = 8192
EIGEN = 16
BINS = 64
CHUNK = 256
CHUNKS = PIXELS // CHUNK
STEP = 512
STEPS = PIXELS // STEP
DEEP = 4
SLOTS = BINS * CAP
PART = CAP // 2
DESTS = 64
DEPTH = 16 * PART


def pack_kernel(weights_hbm, used_hbm, bins_hbm, eigen_hbm, raw_hbm, out_ref,
                weights_ref, used_ref, bins_ref, eigen_ref, raw_ref,
                hot_ref, cum_ref, row_ref, place0, place1, place2, place3, even_ref, odd_ref, slot_ref, sems):
    f32, bf16 = jnp.float32, jnp.bfloat16
    sources = (bins_hbm, eigen_hbm, weights_hbm, used_hbm, raw_hbm)
    targets = (bins_ref, eigen_ref, weights_ref, used_ref, raw_ref)
    loads = [pltpu.make_async_copy(a, b, sems.at[i]) for i, (a, b) in enumerate(zip(sources, targets))]
    for load in loads:
        load.start()
    zero = jnp.zeros((128, 128), f32)

    @pl.loop(0, SLOTS // 128)
    def _(i):
        slot_ref[pl.ds(pl.multiple_of(i * 128, 128), 128), :] = zero
    slot_ref[SLOTS:, :] = jnp.zeros((8, 128), f32)
    loads[0].wait()

    label = lax.broadcasted_iota(jnp.int32, (BINS, 128), 0) + 1
    for j in range(CHUNKS):
        for h in range(2):
            hot_ref[j * BINS:(j + 1) * BINS, h * 128:(h + 1) * 128] = jnp.where(
                bins_ref[2 * j + h:2 * j + h + 1, :] == label, 1.0, 0.0).astype(bf16)
    before = lax.broadcasted_iota(jnp.int32, (CHUNK, CHUNK + 128), 0)
    after = lax.broadcasted_iota(jnp.int32, (CHUNK, CHUNK + 128), 1)
    prefix = jnp.where((before < after) | (after >= CHUNK), 1.0, 0.0).astype(bf16)
    cum_ref[...] = jnp.dot(hot_ref[...], prefix, preferred_element_type=f32)
    carry = jnp.zeros((BINS, 128), f32)
    for j in range(CHUNKS):
        rows = slice(j * BINS, (j + 1) * BINS)
        for h in range(2):
            lanes = slice(h * 128, (h + 1) * 128)
            rank = jnp.sum(hot_ref[rows, lanes].astype(f32) * (cum_ref[rows, lanes] + carry), axis=0, keepdims=True)
            own = bins_ref[2 * j + h:2 * j + h + 1, :]
            row_ref[2 * j + h:2 * j + h + 1, :] = jnp.where(
                own > 0, (own - 1) * CAP + rank.astype(jnp.int32), SLOTS)
        carry = carry + cum_ref[rows, CHUNK:]
    places, values = (place0, place1, place2, place3), (even_ref, odd_ref)

    def fetch(j, k):
        rows = pl.ds(pl.multiple_of(j * (STEP // 128), STEP // 128), STEP // 128)
        return pltpu.make_async_copy(row_ref.at[rows, :], places[k], sems.at[5 + k])

    for k in range(DEEP):
        fetch(k, k).start()
    for load in loads[1:]:
        load.wait()

    in_use = lax.broadcasted_iota(jnp.int32, (EIGEN, FRAMES), 0) < used_ref[...]
    coef = jnp.where(in_use, weights_ref[...], 0.0)
    high = coef.astype(bf16)
    rest = coef - high.astype(f32)
    mid = rest.astype(bf16)
    low = (rest - mid.astype(f32)).astype(bf16)
    weights = jnp.concatenate([high.astype(f32), mid.astype(f32), low.astype(f32)], axis=0).T.astype(bf16)

    def correct(j, target):
        at = pl.ds(pl.multiple_of(j * STEP, STEP), STEP)
        flats = eigen_ref[:, at]
        field = 0.5 + jnp.dot(weights, jnp.concatenate([flats] * 3, axis=0), preferred_element_type=f32)
        value = (raw_ref[:, at].astype(f32) / field).astype(bf16).astype(f32)
        for h in range(STEP // 128):
            part = value[:, h * 128:(h + 1) * 128]
            target[h * 128:(h + 1) * 128, :] = jnp.concatenate([part, part], axis=0).T

    def scatter(source, place_ref):
        for i in range(STEP):
            slot_ref[pl.ds(place_ref[i // 128, i % 128], 1), :] = source[i:i + 1, :]

    correct(0, even_ref)

    @pl.loop(0, STEPS // DEEP)
    def _(i):
        for k in range(DEEP):
            fetch(DEEP * i + k, k).wait()
            scatter(values[k % 2], places[k])

            @pl.when(i < STEPS // DEEP - 1)
            def _():
                fetch(DEEP * (i + 1) + k, k).start()
            correct(jnp.minimum(DEEP * i + k + 1, STEPS - 1), values[(k + 1) % 2])

    left = lax.broadcasted_iota(jnp.int32, (PART, 128), 1) < FRAMES

    @pl.loop(0, BINS // 4)
    def _(z):
        for x in range(4):
            base = (4 * z + x) * CAP
            lo = slot_ref[pl.ds(pl.multiple_of(base, 8), PART), :]
            hi = slot_ref[pl.ds(pl.multiple_of(base + PART, 8), PART), :]
            out_ref[x * 16 + z] = jnp.where(left, lo, hi).astype(bf16)


def pack(weights, used, bins, eigen, raw):
    f32 = jnp.float32
    return pl.pallas_call(
        pack_kernel,
        out_shape=jax.ShapeDtypeStruct((DESTS, PART, 128), jnp.bfloat16),
        in_specs=[pl.BlockSpec(memory_space=pltpu.HBM)] * 5,
        out_specs=pl.BlockSpec(memory_space=pltpu.VMEM),
        scratch_shapes=[
            pltpu.VMEM((EIGEN, FRAMES), f32),
            pltpu.VMEM((1, FRAMES), jnp.int32),
            pltpu.VMEM((PIXELS // 128, 128), jnp.int32),
            pltpu.VMEM((EIGEN, PIXELS), jnp.bfloat16),
            pltpu.VMEM((FRAMES, PIXELS), jnp.bfloat16),
            pltpu.VMEM((CHUNKS * BINS, CHUNK), jnp.bfloat16),
            pltpu.VMEM((CHUNKS * BINS, CHUNK + 128), f32),
            pltpu.VMEM((PIXELS // 128, 128), jnp.int32),
            *[pltpu.SMEM((STEP // 128, 128), jnp.int32)] * DEEP,
            pltpu.VMEM((STEP, 128), f32),
            pltpu.VMEM((STEP, 128), f32),
            pltpu.VMEM((SLOTS + 8, 128), f32),
            pltpu.SemaphoreType.DMA((5 + DEEP,)),
        ],
        compiler_params=pltpu.CompilerParams(vmem_limit_bytes=24 << 20),
        name="pack",
    )(*(pltpu.with_memory_space_constraint(a, pltpu.HBM) for a in (weights, used, bins, eigen, raw)))


def gram_kernel(core_ref, mine_ref, next_ref, last_ref, keep_ref, send_ref, own_ref):
    f32, bf16 = jnp.float32, jnp.bfloat16
    first = core_ref[0] == 0
    left = lax.broadcasted_iota(jnp.int32, (1, 128), 1) < FRAMES
    ones = jnp.ones((8, DEPTH), bf16)

    def matrix(ref):
        return jnp.concatenate([ref[x * DEPTH:(x + 1) * DEPTH, :] for x in range(4)], axis=1)

    def fold(even_top, even_low, odd_top, odd_low):
        return jnp.where(left, even_top, odd_low) + pltpu.roll(
            jnp.where(left, odd_top, even_low), FRAMES, 1)

    def product(a, b, group):
        full = lax.dot_general(a, b, (((0,), (0,)), ((), ())), preferred_element_type=f32)
        for x in range(4):
            top, low = slice(x * 128, x * 128 + 64), slice(x * 128 + 64, x * 128 + 128)
            for e in range(2):
                even, odd = slice(e * 256, e * 256 + 128), slice(e * 256 + 128, e * 256 + 256)
                part = fold(full[top, even], full[low, even], full[top, odd], full[low, odd])
                lanes = slice(group * 256 + e * 128, group * 256 + e * 128 + 128)
                keep_ref[x, :, lanes] = jnp.where(first, part[:32], part[32:])
                send_ref[x * 32:(x + 1) * 32, lanes] = jnp.where(first, part[32:], part[:32])

    def total(b, group):
        full = jnp.dot(ones, b, preferred_element_type=f32)
        for e in range(2):
            even, odd = full[:, e * 256:e * 256 + 128], full[:, e * 256 + 128:e * 256 + 256]
            lanes = slice(group * 256 + e * 128, group * 256 + e * 128 + 128)
            part = fold(even, even, odd, odd)
            own_ref[:, lanes] = part
            send_ref[128:, lanes] = part

    mine, after, prior = matrix(mine_ref), matrix(next_ref), matrix(last_ref)
    product(mine, mine, 1)
    product(mine, prior, 0)
    product(mine, after, 2)
    product(prior, after, 3)
    total(prior, 0)
    total(mine, 1)
    total(after, 2)
    hits = jnp.where(mine_ref[:DEPTH, :].astype(f32) != 0.0, 1.0, 0.0).astype(bf16)
    hits = jnp.dot(ones, hits, preferred_element_type=f32)
    hits = hits + pltpu.roll(hits, FRAMES, 1)
    for e in range(2):
        own_ref[:, 768 + e * 128:896 + e * 128] = hits
        send_ref[128:, 768 + e * 128:896 + e * 128] = hits


def gram(core, mine, after, prior):
    f32 = jnp.float32
    return pl.pallas_call(
        gram_kernel,
        out_shape=(jax.ShapeDtypeStruct((4, 32, 1024), f32),
                   jax.ShapeDtypeStruct((136, 1024), f32),
                   jax.ShapeDtypeStruct((8, 1024), f32)),
        in_specs=[pl.BlockSpec(memory_space=pltpu.SMEM)] + [pl.BlockSpec(memory_space=pltpu.VMEM)] * 3,
        out_specs=(pl.BlockSpec(memory_space=pltpu.VMEM),) * 3,
        compiler_params=pltpu.CompilerParams(vmem_limit_bytes=24 << 20),
        name="gram",
    )(core, mine, after, prior)


def scale_kernel(core_ref, keep_ref, got_ref, own_ref, rows_ref):
    first = core_ref[0] == 0
    sums = own_ref[...] + got_ref[128:, :]
    count = sums[0:1, 768:896]
    count = jnp.concatenate([count, count], axis=1)

    def column(group):
        tall = [jnp.broadcast_to(sums[0:1, group * 256 + e * 128:group * 256 + e * 128 + 128], (128, 128)).T
                for e in range(2)]
        tall = jnp.concatenate(tall, axis=0)
        parts = []
        for x in range(4):
            part = jnp.where(first, tall[x * 64:x * 64 + 32], tall[x * 64 + 32:x * 64 + 64])
            parts.append(jnp.concatenate([part, part], axis=1))
        return parts

    mine, prior = column(1), column(0)
    for x in range(4):
        for group in range(4):
            lanes = slice(group * 256, group * 256 + 256)
            value = keep_ref[x, :, lanes] + got_ref[x * 32:(x + 1) * 32, lanes]
            if group < 3:
                rows_ref[x, :, lanes] = count * value / (mine[x] * sums[0:1, lanes])
            else:
                rows_ref[x, :, lanes] = count * value / (prior[x] * sums[0:1, 512:768])


def scale(core, keep, got, own):
    f32 = jnp.float32
    return pl.pallas_call(
        scale_kernel,
        out_shape=jax.ShapeDtypeStruct((4, 32, 1024), f32),
        in_specs=[pl.BlockSpec(memory_space=pltpu.SMEM)] + [pl.BlockSpec(memory_space=pltpu.VMEM)] * 3,
        out_specs=pl.BlockSpec(memory_space=pltpu.VMEM),
        compiler_params=pltpu.CompilerParams(vmem_limit_bytes=8 << 20),
        name="scale",
    )(core, keep, got, own)


def place_kernel(at_ref, rows_ref, swap_ref, far_ref, out_ref):
    core = at_ref[0]
    own, other = (pl.ds(pl.multiple_of(c * 32, 32), 32) for c in (core, 1 - core))
    for group in range(4):
        lanes = pl.ds(pl.multiple_of(at_ref[1 + group] * 256, 256), 256)
        source = slice(group * 256, (group + 1) * 256)
        for b in range(2):
            if group < 3:
                out_ref[b, own, lanes] = rows_ref[2 * core + b, :, source]
                out_ref[b, other, lanes] = swap_ref[b, :, source]
            else:
                out_ref[b, own, lanes] = far_ref[b]
                out_ref[b, other, lanes] = far_ref[2 + b]


def place(at, rows, swap, far):
    return pl.pallas_call(
        place_kernel,
        out_shape=jax.ShapeDtypeStruct((2, 64, 1024), jnp.float32),
        in_specs=[pl.BlockSpec(memory_space=pltpu.SMEM)] + [pl.BlockSpec(memory_space=pltpu.VMEM)] * 3,
        out_specs=pl.BlockSpec(memory_space=pltpu.VMEM),
        compiler_params=pltpu.CompilerParams(vmem_limit_bytes=8 << 20),
        name="place",
    )(at, rows, swap, far)


SWAP = [(0, 1), (1, 0)]
NEAR = [(0, 1), (1, 0), (2, 3), (3, 2)]
WRAP = [(0, 3), (1, 2), (2, 1), (3, 0)]


def shards(raw_frames, eigen_flats, weights, flat_count, bin_map):
    core = lax.axis_index("c").astype(jnp.int32)
    row = lax.axis_index("y").astype(jnp.int32)
    packed = pack(weights.T, flat_count[None, :], bin_map.reshape(PIXELS // 128, 128), eigen_flats, raw_frames)
    mine = lax.all_to_all(packed, ("x", "z"), 0, 0, tiled=True).reshape(4 * DEPTH, 128)
    prior = lax.ppermute(mine, "y", NEAR)
    after = lax.ppermute(mine, "y", WRAP)
    keep, send, own = gram(core[None], mine, after, prior)
    got = lax.ppermute(send, "c", SWAP)
    first, second, at, rows = lax.optimization_barrier(
        (2 * core, 2 - 2 * core, jnp.stack([core, row ^ 1, row, 3 - row, (row + 2) % 4]), scale(core[None], keep, got, own)))
    rows = lax.all_to_all(rows, "x", 0, 0, tiled=True)
    swap = lax.ppermute(lax.dynamic_slice_in_dim(rows, second, 2, 0, allow_negative_indices=False), "c", SWAP)
    far = jnp.concatenate([lax.dynamic_slice(rows, (first, 0, 768), (2, 32, 256), allow_negative_indices=False), swap[:, :, 768:]], axis=0)
    far = lax.ppermute(far, "y", NEAR)
    return place(at, rows, swap, far)


def solution(mesh):
    split = Mesh(mesh.devices.reshape(16, 2, 4, 4), ("z", "c", "y", "x"))
    return jax.shard_map(
        shards,
        mesh=split,
        in_specs=(P(("y", "x"), ("z", "c")), P(None, ("z", "c")), P(("y", "x"), None), P(("y", "x")), P(("z", "c"))),
        out_specs=P(("z", "c"), ("y", "x"), None),
        check_vma=False,
    )
```

```python
import jax, jax.numpy as jnp
from jax import lax
from jax.experimental import pallas as pl
from jax.experimental.pallas import tpu as pltpu
from jax.sharding import Mesh, PartitionSpec as P

CAP = 96
FRAMES = 64
PIXELS = 8192
EIGEN = 16
BINS = 64
CHUNK = 256
CHUNKS = PIXELS // CHUNK
STEP = 512
STEPS = PIXELS // STEP
DEEP = 4
SLOTS = BINS * CAP
PART = CAP // 2
DESTS = 64
DEPTH = 16 * PART


def pack_kernel(weights_hbm, used_hbm, bins_hbm, eigen_hbm, raw_hbm, out_ref,
                weights_ref, used_ref, bins_ref, eigen_ref, raw_ref,
                hot_ref, cum_ref, row_ref, place0, place1, place2, place3, even_ref, odd_ref, slot_ref, sems):
    f32, bf16 = jnp.float32, jnp.bfloat16
    sources = (bins_hbm, eigen_hbm, weights_hbm, used_hbm, raw_hbm)
    targets = (bins_ref, eigen_ref, weights_ref, used_ref, raw_ref)
    loads = [pltpu.make_async_copy(a, b, sems.at[i]) for i, (a, b) in enumerate(zip(sources, targets))]
    for load in loads:
        load.start()
    zero = jnp.zeros((128, 128), f32)

    @pl.loop(0, SLOTS // 128)
    def _(i):
        slot_ref[pl.ds(pl.multiple_of(i * 128, 128), 128), :] = zero
    slot_ref[SLOTS:, :] = jnp.zeros((8, 128), f32)
    loads[0].wait()

    label = lax.broadcasted_iota(jnp.int32, (BINS, 128), 0) + 1
    for j in range(CHUNKS):
        for h in range(2):
            hot_ref[j * BINS:(j + 1) * BINS, h * 128:(h + 1) * 128] = jnp.where(
                bins_ref[2 * j + h:2 * j + h + 1, :] == label, 1.0, 0.0).astype(bf16)
    before = lax.broadcasted_iota(jnp.int32, (CHUNK, CHUNK + 128), 0)
    after = lax.broadcasted_iota(jnp.int32, (CHUNK, CHUNK + 128), 1)
    prefix = jnp.where((before < after) | (after >= CHUNK), 1.0, 0.0).astype(bf16)
    cum_ref[...] = jnp.dot(hot_ref[...], prefix, preferred_element_type=f32)
    carry = jnp.zeros((BINS, 128), f32)
    for j in range(CHUNKS):
        rows = slice(j * BINS, (j + 1) * BINS)
        for h in range(2):
            lanes = slice(h * 128, (h + 1) * 128)
            rank = jnp.sum(hot_ref[rows, lanes].astype(f32) * (cum_ref[rows, lanes] + carry), axis=0, keepdims=True)
            own = bins_ref[2 * j + h:2 * j + h + 1, :]
            row_ref[2 * j + h:2 * j + h + 1, :] = jnp.where(
                own > 0, (own - 1) * CAP + rank.astype(jnp.int32), SLOTS)
        carry = carry + cum_ref[rows, CHUNK:]
    places, values = (place0, place1, place2, place3), (even_ref, odd_ref)

    def fetch(j, k):
        rows = pl.ds(pl.multiple_of(j * (STEP // 128), STEP // 128), STEP // 128)
        return pltpu.make_async_copy(row_ref.at[rows, :], places[k], sems.at[5 + k])

    for k in range(DEEP):
        fetch(k, k).start()
    for load in loads[1:]:
        load.wait()

    in_use = lax.broadcasted_iota(jnp.int32, (EIGEN, FRAMES), 0) < used_ref[...]
    coef = jnp.where(in_use, weights_ref[...], 0.0)
    high = coef.astype(bf16)
    rest = coef - high.astype(f32)
    mid = rest.astype(bf16)
    low = (rest - mid.astype(f32)).astype(bf16)
    weights = jnp.concatenate([high.astype(f32), mid.astype(f32), low.astype(f32)], axis=0).T.astype(bf16)

    def correct(j, target):
        at = pl.ds(pl.multiple_of(j * STEP, STEP), STEP)
        flats = eigen_ref[:, at]
        field = 0.5 + jnp.dot(weights, jnp.concatenate([flats] * 3, axis=0), preferred_element_type=f32)
        value = (raw_ref[:, at].astype(f32) / field).astype(bf16).astype(f32)
        for h in range(STEP // 128):
            part = value[:, h * 128:(h + 1) * 128]
            target[h * 128:(h + 1) * 128, :] = jnp.concatenate([part, part], axis=0).T

    def scatter(source, place_ref):
        for i in range(STEP):
            slot_ref[pl.ds(place_ref[i // 128, i % 128], 1), :] = source[i:i + 1, :]

    correct(0, even_ref)

    @pl.loop(0, STEPS // DEEP)
    def _(i):
        for k in range(DEEP):
            fetch(DEEP * i + k, k).wait()
            scatter(values[k % 2], places[k])

            @pl.when(i < STEPS // DEEP - 1)
            def _():
                fetch(DEEP * (i + 1) + k, k).start()
            correct(jnp.minimum(DEEP * i + k + 1, STEPS - 1), values[(k + 1) % 2])

    left = lax.broadcasted_iota(jnp.int32, (PART, 128), 1) < FRAMES

    @pl.loop(0, BINS // 4)
    def _(z):
        for x in range(4):
            base = (4 * z + x) * CAP
            lo = slot_ref[pl.ds(pl.multiple_of(base, 8), PART), :]
            hi = slot_ref[pl.ds(pl.multiple_of(base + PART, 8), PART), :]
            out_ref[x * 16 + z] = jnp.where(left, lo, hi).astype(bf16)


def pack(weights, used, bins, eigen, raw):
    f32 = jnp.float32
    return pl.pallas_call(
        pack_kernel,
        out_shape=jax.ShapeDtypeStruct((DESTS, PART, 128), jnp.bfloat16),
        in_specs=[pl.BlockSpec(memory_space=pltpu.HBM)] * 5,
        out_specs=pl.BlockSpec(memory_space=pltpu.VMEM),
        scratch_shapes=[
            pltpu.VMEM((EIGEN, FRAMES), f32),
            pltpu.VMEM((1, FRAMES), jnp.int32),
            pltpu.VMEM((PIXELS // 128, 128), jnp.int32),
            pltpu.VMEM((EIGEN, PIXELS), jnp.bfloat16),
            pltpu.VMEM((FRAMES, PIXELS), jnp.bfloat16),
            pltpu.VMEM((CHUNKS * BINS, CHUNK), jnp.bfloat16),
            pltpu.VMEM((CHUNKS * BINS, CHUNK + 128), f32),
            pltpu.VMEM((PIXELS // 128, 128), jnp.int32),
            *[pltpu.SMEM((STEP // 128, 128), jnp.int32)] * DEEP,
            pltpu.VMEM((STEP, 128), f32),
            pltpu.VMEM((STEP, 128), f32),
            pltpu.VMEM((SLOTS + 8, 128), f32),
            pltpu.SemaphoreType.DMA((5 + DEEP,)),
        ],
        compiler_params=pltpu.CompilerParams(vmem_limit_bytes=24 << 20),
        name="pack",
    )(*(pltpu.with_memory_space_constraint(a, pltpu.HBM) for a in (weights, used, bins, eigen, raw)))


def matrix(ref):
    return jnp.concatenate([ref[x * DEPTH:(x + 1) * DEPTH, :] for x in range(4)], axis=1)


def fold(even_top, even_low, odd_top, odd_low):
    left = lax.broadcasted_iota(jnp.int32, (1, 128), 1) < FRAMES
    return jnp.where(left, even_top, odd_low) + pltpu.roll(
        jnp.where(left, odd_top, even_low), FRAMES, 1)


def products(a, b):
    full = lax.dot_general(a, b, (((0,), (0,)), ((), ())), preferred_element_type=jnp.float32)
    for x in range(4):
        top, low = slice(x * 128, x * 128 + 64), slice(x * 128 + 64, x * 128 + 128)
        for e in range(2):
            even, odd = slice(e * 256, e * 256 + 128), slice(e * 256 + 128, e * 256 + 256)
            yield x, e, fold(full[top, even], full[low, even], full[top, odd], full[low, odd])


def totals(b):
    full = jnp.dot(jnp.ones((8, DEPTH), jnp.bfloat16), b, preferred_element_type=jnp.float32)
    for e in range(2):
        even, odd = full[:, e * 256:e * 256 + 128], full[:, e * 256 + 128:e * 256 + 256]
        yield e, fold(even, even, odd, odd)


def cross_kernel(core_ref, near_ref, wrap_ref, far_ref):
    first = core_ref[0] == 0
    near, wrap = matrix(near_ref), matrix(wrap_ref)
    for x, e, part in products(near, wrap):
        lanes = slice(e * 128, e * 128 + 128)
        far_ref[0, x * 32:(x + 1) * 32, lanes] = jnp.where(first, part[:32], part[32:])
        far_ref[1, x * 32:(x + 1) * 32, lanes] = jnp.where(first, part[32:], part[:32])
    for e, part in totals(wrap):
        for half in range(2):
            far_ref[half, 128:, e * 128:e * 128 + 128] = part


def cross(core, near, wrap):
    return pl.pallas_call(
        cross_kernel,
        out_shape=jax.ShapeDtypeStruct((2, 136, 256), jnp.float32),
        in_specs=[pl.BlockSpec(memory_space=pltpu.SMEM)] + [pl.BlockSpec(memory_space=pltpu.VMEM)] * 2,
        out_specs=pl.BlockSpec(memory_space=pltpu.VMEM),
        compiler_params=pltpu.CompilerParams(vmem_limit_bytes=16 << 20),
        name="cross",
    )(core, near, wrap)


def gram_kernel(core_ref, mine_ref, near_ref, wrap_ref, keep_ref, send_ref, own_ref):
    f32, bf16 = jnp.float32, jnp.bfloat16
    first = core_ref[0] == 0
    mine = matrix(mine_ref)
    for group, ref in enumerate((near_ref, mine_ref, wrap_ref)):
        other = matrix(ref)
        for x, e, part in products(mine, other):
            lanes = slice(group * 256 + e * 128, group * 256 + e * 128 + 128)
            keep_ref[x, :, lanes] = jnp.where(first, part[:32], part[32:])
            send_ref[x * 32:(x + 1) * 32, lanes] = jnp.where(first, part[32:], part[:32])
        for e, part in totals(other):
            lanes = slice(group * 256 + e * 128, group * 256 + e * 128 + 128)
            own_ref[:8, lanes] = part
            send_ref[128:136, lanes] = part
    hits = jnp.where(mine_ref[:DEPTH, :].astype(f32) != 0.0, 1.0, 0.0).astype(bf16)
    hits = jnp.dot(jnp.ones((8, DEPTH), bf16), hits, preferred_element_type=f32)
    hits = hits + pltpu.roll(hits, FRAMES, 1)
    hits = jnp.concatenate([hits] * 6, axis=1)
    own_ref[8:, :] = hits
    send_ref[136:, :] = hits


def gram(core, mine, near, wrap):
    f32 = jnp.float32
    return pl.pallas_call(
        gram_kernel,
        out_shape=(jax.ShapeDtypeStruct((4, 32, 768), f32),
                   jax.ShapeDtypeStruct((144, 768), f32),
                   jax.ShapeDtypeStruct((16, 768), f32)),
        in_specs=[pl.BlockSpec(memory_space=pltpu.SMEM)] + [pl.BlockSpec(memory_space=pltpu.VMEM)] * 3,
        out_specs=(pl.BlockSpec(memory_space=pltpu.VMEM),) * 3,
        compiler_params=pltpu.CompilerParams(vmem_limit_bytes=24 << 20),
        name="gram",
    )(core, mine, near, wrap)


def scale_kernel(core_ref, keep_ref, got_ref, own_ref, far_ref, far_got_ref, rows_ref):
    first = core_ref[0] == 0
    sums = own_ref[...] + got_ref[128:, :]
    far_sums = far_ref[0, 128:, :] + far_got_ref[128:, :]
    count = sums[8:9, :256]
    tall = [jnp.broadcast_to(sums[0:1, 256 + e * 128:384 + e * 128], (128, 128)).T for e in range(2)]
    tall = jnp.concatenate(tall, axis=0)
    for x in range(4):
        part = jnp.where(first, tall[x * 64:x * 64 + 32], tall[x * 64 + 32:x * 64 + 64])
        mine = jnp.concatenate([part, part], axis=1)
        rows = slice(x * 32, (x + 1) * 32)
        for group in range(3):
            lanes = slice(group * 256, group * 256 + 256)
            value = keep_ref[x, :, lanes] + got_ref[rows, lanes]
            rows_ref[x, :, lanes] = count * value / (mine * sums[0:1, lanes])
        value = far_ref[0, rows, :] + far_got_ref[rows, :]
        rows_ref[x, :, 768:] = count * value / (mine * far_sums[0:1, :])


def scale(core, keep, got, own, far, far_got):
    return pl.pallas_call(
        scale_kernel,
        out_shape=jax.ShapeDtypeStruct((4, 32, 1024), jnp.float32),
        in_specs=[pl.BlockSpec(memory_space=pltpu.SMEM)] + [pl.BlockSpec(memory_space=pltpu.VMEM)] * 5,
        out_specs=pl.BlockSpec(memory_space=pltpu.VMEM),
        compiler_params=pltpu.CompilerParams(vmem_limit_bytes=8 << 20),
        name="scale",
    )(core, keep, got, own, far, far_got)


def place_kernel(at_ref, rows_ref, swap_ref, out_ref):
    core = at_ref[0]
    own, other = (pl.ds(pl.multiple_of(c * 32, 32), 32) for c in (core, 1 - core))
    for group in range(4):
        lanes = pl.ds(pl.multiple_of(at_ref[1 + group] * 256, 256), 256)
        source = slice(group * 256, (group + 1) * 256)
        for b in range(2):
            out_ref[b, own, lanes] = rows_ref[2 * core + b, :, source]
            out_ref[b, other, lanes] = swap_ref[b, :, source]


def place(at, rows, swap):
    return pl.pallas_call(
        place_kernel,
        out_shape=jax.ShapeDtypeStruct((2, 64, 1024), jnp.float32),
        in_specs=[pl.BlockSpec(memory_space=pltpu.SMEM)] + [pl.BlockSpec(memory_space=pltpu.VMEM)] * 2,
        out_specs=pl.BlockSpec(memory_space=pltpu.VMEM),
        compiler_params=pltpu.CompilerParams(vmem_limit_bytes=8 << 20),
        name="place",
    )(at, rows, swap)


SWAP = [(0, 1), (1, 0)]
NEAR = [(0, 1), (1, 0), (2, 3), (3, 2)]
WRAP = [(0, 3), (1, 2), (2, 1), (3, 0)]


def shards(raw_frames, eigen_flats, weights, flat_count, bin_map):
    core = lax.axis_index("c").astype(jnp.int32)
    row = lax.axis_index("y").astype(jnp.int32)
    packed = pack(weights.T, flat_count[None, :], bin_map.reshape(PIXELS // 128, 128), eigen_flats, raw_frames)
    mine = lax.all_to_all(packed, ("x", "z"), 0, 0, tiled=True).reshape(4 * DEPTH, 128)
    near = lax.ppermute(mine, "y", NEAR)
    wrap = lax.ppermute(mine, "y", WRAP)
    far = lax.ppermute(cross(core[None], near, wrap), "y", NEAR)
    keep, send, own = gram(core[None], mine, near, wrap)
    got = lax.ppermute(send, "c", SWAP)
    far_got = lax.ppermute(far[1], "c", SWAP)
    at, second, rows = lax.optimization_barrier(
        (jnp.stack([core, row ^ 1, row, 3 - row, (row + 2) % 4]), 2 - 2 * core,
         scale(core[None], keep, got, own, far, far_got)))
    rows = lax.all_to_all(rows, "x", 0, 0, tiled=True)
    swap = lax.ppermute(lax.dynamic_slice_in_dim(rows, second, 2, 0, allow_negative_indices=False), "c", SWAP)
    return place(at, rows, swap)


def solution(mesh):
    split = Mesh(mesh.devices.reshape(16, 2, 4, 4), ("z", "c", "y", "x"))
    return jax.shard_map(
        shards,
        mesh=split,
        in_specs=(P(("y", "x"), ("z", "c")), P(None, ("z", "c")), P(("y", "x"), None), P(("y", "x")), P(("z", "c"))),
        out_specs=P(("z", "c"), ("y", "x"), None),
        check_vma=False,
    )
```

```python
import jax, jax.numpy as jnp
from jax import lax
from jax.experimental import pallas as pl
from jax.experimental.pallas import tpu as pltpu
from jax.sharding import Mesh, PartitionSpec as P

CAP = 96
FRAMES = 64
PIXELS = 8192
EIGEN = 16
BINS = 64
CHUNK = 256
CHUNKS = PIXELS // CHUNK
STEP = 512
STEPS = PIXELS // STEP
DEEP = 4
SLOTS = BINS * CAP
PART = CAP // 2
DESTS = 64
DEPTH = 16 * PART


def pack_kernel(weights_hbm, used_hbm, bins_hbm, eigen_hbm, raw_hbm, out_ref,
                weights_ref, used_ref, bins_ref, eigen_ref, raw_ref,
                hot_ref, cum_ref, row_ref, place0, place1, place2, place3, even_ref, odd_ref, slot_ref, sems):
    f32, bf16 = jnp.float32, jnp.bfloat16
    sources = (bins_hbm, eigen_hbm, weights_hbm, used_hbm, raw_hbm)
    targets = (bins_ref, eigen_ref, weights_ref, used_ref, raw_ref)
    loads = [pltpu.make_async_copy(a, b, sems.at[i]) for i, (a, b) in enumerate(zip(sources, targets))]
    for load in loads:
        load.start()
    zero = jnp.zeros((128, 128), f32)

    @pl.loop(0, SLOTS // 128)
    def _(i):
        slot_ref[pl.ds(pl.multiple_of(i * 128, 128), 128), :] = zero
    slot_ref[SLOTS:, :] = jnp.zeros((8, 128), f32)
    loads[0].wait()

    label = lax.broadcasted_iota(jnp.int32, (BINS, 128), 0) + 1
    for j in range(CHUNKS):
        for h in range(2):
            hot_ref[j * BINS:(j + 1) * BINS, h * 128:(h + 1) * 128] = jnp.where(
                bins_ref[2 * j + h:2 * j + h + 1, :] == label, 1.0, 0.0).astype(bf16)
    before = lax.broadcasted_iota(jnp.int32, (CHUNK, CHUNK + 128), 0)
    after = lax.broadcasted_iota(jnp.int32, (CHUNK, CHUNK + 128), 1)
    prefix = jnp.where((before < after) | (after >= CHUNK), 1.0, 0.0).astype(bf16)
    cum_ref[...] = jnp.dot(hot_ref[...], prefix, preferred_element_type=f32)
    carry = jnp.zeros((BINS, 128), f32)
    for j in range(CHUNKS):
        rows = slice(j * BINS, (j + 1) * BINS)
        for h in range(2):
            lanes = slice(h * 128, (h + 1) * 128)
            rank = jnp.sum(hot_ref[rows, lanes].astype(f32) * (cum_ref[rows, lanes] + carry), axis=0, keepdims=True)
            own = bins_ref[2 * j + h:2 * j + h + 1, :]
            row_ref[2 * j + h:2 * j + h + 1, :] = jnp.where(
                own > 0, (own - 1) * CAP + rank.astype(jnp.int32), SLOTS)
        carry = carry + cum_ref[rows, CHUNK:]
    places, values = (place0, place1, place2, place3), (even_ref, odd_ref)

    def fetch(j, k):
        rows = pl.ds(pl.multiple_of(j * (STEP // 128), STEP // 128), STEP // 128)
        return pltpu.make_async_copy(row_ref.at[rows, :], places[k], sems.at[5 + k])

    for k in range(DEEP):
        fetch(k, k).start()
    for load in loads[1:]:
        load.wait()

    in_use = lax.broadcasted_iota(jnp.int32, (EIGEN, FRAMES), 0) < used_ref[...]
    coef = jnp.where(in_use, weights_ref[...], 0.0)
    high = coef.astype(bf16)
    rest = coef - high.astype(f32)
    mid = rest.astype(bf16)
    low = (rest - mid.astype(f32)).astype(bf16)
    weights = jnp.concatenate([high.astype(f32), mid.astype(f32), low.astype(f32)], axis=0).T.astype(bf16)

    def correct(j, target):
        at = pl.ds(pl.multiple_of(j * STEP, STEP), STEP)
        flats = eigen_ref[:, at]
        field = 0.5 + jnp.dot(weights, jnp.concatenate([flats] * 3, axis=0), preferred_element_type=f32)
        value = (raw_ref[:, at].astype(f32) / field).astype(bf16).astype(f32)
        for h in range(STEP // 128):
            part = value[:, h * 128:(h + 1) * 128]
            target[h * 128:(h + 1) * 128, :] = jnp.concatenate([part, part], axis=0).T

    def scatter(source, place_ref):
        for i in range(STEP):
            slot_ref[pl.ds(place_ref[i // 128, i % 128], 1), :] = source[i:i + 1, :]

    correct(0, even_ref)

    @pl.loop(0, STEPS // DEEP)
    def _(i):
        for k in range(DEEP):
            fetch(DEEP * i + k, k).wait()
            scatter(values[k % 2], places[k])

            @pl.when(i < STEPS // DEEP - 1)
            def _():
                fetch(DEEP * (i + 1) + k, k).start()
            correct(jnp.minimum(DEEP * i + k + 1, STEPS - 1), values[(k + 1) % 2])

    left = lax.broadcasted_iota(jnp.int32, (PART, 128), 1) < FRAMES

    @pl.loop(0, BINS // 4)
    def _(z):
        for x in range(4):
            base = (4 * z + x) * CAP
            lo = slot_ref[pl.ds(pl.multiple_of(base, 8), PART), :]
            hi = slot_ref[pl.ds(pl.multiple_of(base + PART, 8), PART), :]
            out_ref[x * 16 + z] = jnp.where(left, lo, hi).astype(bf16)


def pack(weights, used, bins, eigen, raw):
    f32 = jnp.float32
    return pl.pallas_call(
        pack_kernel,
        out_shape=jax.ShapeDtypeStruct((DESTS, PART, 128), jnp.bfloat16),
        in_specs=[pl.BlockSpec(memory_space=pltpu.HBM)] * 5,
        out_specs=pl.BlockSpec(memory_space=pltpu.VMEM),
        scratch_shapes=[
            pltpu.VMEM((EIGEN, FRAMES), f32),
            pltpu.VMEM((1, FRAMES), jnp.int32),
            pltpu.VMEM((PIXELS // 128, 128), jnp.int32),
            pltpu.VMEM((EIGEN, PIXELS), jnp.bfloat16),
            pltpu.VMEM((FRAMES, PIXELS), jnp.bfloat16),
            pltpu.VMEM((CHUNKS * BINS, CHUNK), jnp.bfloat16),
            pltpu.VMEM((CHUNKS * BINS, CHUNK + 128), f32),
            pltpu.VMEM((PIXELS // 128, 128), jnp.int32),
            *[pltpu.SMEM((STEP // 128, 128), jnp.int32)] * DEEP,
            pltpu.VMEM((STEP, 128), f32),
            pltpu.VMEM((STEP, 128), f32),
            pltpu.VMEM((SLOTS + 8, 128), f32),
            pltpu.SemaphoreType.DMA((5 + DEEP,)),
        ],
        compiler_params=pltpu.CompilerParams(vmem_limit_bytes=24 << 20),
        name="pack",
    )(*(pltpu.with_memory_space_constraint(a, pltpu.HBM) for a in (weights, used, bins, eigen, raw)))


def matrix(ref):
    return jnp.concatenate([ref[x * DEPTH:(x + 1) * DEPTH, :] for x in range(4)], axis=1)


def fold(even_top, even_low, odd_top, odd_low):
    left = lax.broadcasted_iota(jnp.int32, (1, 128), 1) < FRAMES
    return jnp.where(left, even_top, odd_low) + pltpu.roll(
        jnp.where(left, odd_top, even_low), FRAMES, 1)


def products(a, b):
    full = lax.dot_general(a, b, (((0,), (0,)), ((), ())), preferred_element_type=jnp.float32)
    for x in range(4):
        top, low = slice(x * 128, x * 128 + 64), slice(x * 128 + 64, x * 128 + 128)
        for e in range(2):
            even, odd = slice(e * 256, e * 256 + 128), slice(e * 256 + 128, e * 256 + 256)
            yield x, e, fold(full[top, even], full[low, even], full[top, odd], full[low, odd])


def totals(b):
    full = jnp.dot(jnp.ones((8, DEPTH), jnp.bfloat16), b, preferred_element_type=jnp.float32)
    for e in range(2):
        even, odd = full[:, e * 256:e * 256 + 128], full[:, e * 256 + 128:e * 256 + 256]
        yield e, fold(even, even, odd, odd)


def cross_kernel(core_ref, near_ref, wrap_ref, same_ref, flip_ref):
    first = core_ref[0] == 0
    near, wrap = matrix(near_ref), matrix(wrap_ref)
    for x, e, part in products(near, wrap):
        lanes = slice(e * 128, e * 128 + 128)
        same_ref[x * 32:(x + 1) * 32, lanes] = jnp.where(first, part[:32], part[32:])
        flip_ref[x * 32:(x + 1) * 32, lanes] = jnp.where(first, part[32:], part[:32])
    for e, part in totals(wrap):
        same_ref[128:, e * 128:e * 128 + 128] = part
        flip_ref[128:, e * 128:e * 128 + 128] = part


def cross(core, near, wrap):
    return pl.pallas_call(
        cross_kernel,
        out_shape=(jax.ShapeDtypeStruct((136, 256), jnp.float32),) * 2,
        in_specs=[pl.BlockSpec(memory_space=pltpu.SMEM)] + [pl.BlockSpec(memory_space=pltpu.VMEM)] * 2,
        out_specs=(pl.BlockSpec(memory_space=pltpu.VMEM),) * 2,
        compiler_params=pltpu.CompilerParams(vmem_limit_bytes=16 << 20),
        name="cross",
    )(core, near, wrap)


def gram_kernel(core_ref, mine_ref, near_ref, wrap_ref, keep_ref, send_ref, own_ref):
    f32, bf16 = jnp.float32, jnp.bfloat16
    first = core_ref[0] == 0
    mine = matrix(mine_ref)
    for group, ref in enumerate((near_ref, mine_ref, wrap_ref)):
        other = matrix(ref)
        for x, e, part in products(mine, other):
            lanes = slice(group * 256 + e * 128, group * 256 + e * 128 + 128)
            keep_ref[x, :, lanes] = jnp.where(first, part[:32], part[32:])
            send_ref[x * 32:(x + 1) * 32, lanes] = jnp.where(first, part[32:], part[:32])
        for e, part in totals(other):
            lanes = slice(group * 256 + e * 128, group * 256 + e * 128 + 128)
            own_ref[:8, lanes] = part
            send_ref[128:136, lanes] = part
    hits = jnp.where(mine_ref[:DEPTH, :].astype(f32) != 0.0, 1.0, 0.0).astype(bf16)
    hits = jnp.dot(jnp.ones((8, DEPTH), bf16), hits, preferred_element_type=f32)
    hits = hits + pltpu.roll(hits, FRAMES, 1)
    hits = jnp.concatenate([hits] * 6, axis=1)
    own_ref[8:, :] = hits
    send_ref[136:, :] = hits


def gram(core, mine, near, wrap):
    f32 = jnp.float32
    return pl.pallas_call(
        gram_kernel,
        out_shape=(jax.ShapeDtypeStruct((4, 32, 768), f32),
                   jax.ShapeDtypeStruct((144, 768), f32),
                   jax.ShapeDtypeStruct((16, 768), f32)),
        in_specs=[pl.BlockSpec(memory_space=pltpu.SMEM)] + [pl.BlockSpec(memory_space=pltpu.VMEM)] * 3,
        out_specs=(pl.BlockSpec(memory_space=pltpu.VMEM),) * 3,
        compiler_params=pltpu.CompilerParams(vmem_limit_bytes=24 << 20),
        name="gram",
    )(core, mine, near, wrap)


def scale_kernel(core_ref, keep_ref, got_ref, own_ref, far_ref, far_got_ref, rows_ref):
    first = core_ref[0] == 0
    sums = own_ref[...] + got_ref[128:, :]
    far_sums = far_ref[128:, :] + far_got_ref[128:, :]
    count = sums[8:9, :256]
    tall = [jnp.broadcast_to(sums[0:1, 256 + e * 128:384 + e * 128], (128, 128)).T for e in range(2)]
    tall = jnp.concatenate(tall, axis=0)
    for x in range(4):
        part = jnp.where(first, tall[x * 64:x * 64 + 32], tall[x * 64 + 32:x * 64 + 64])
        mine = jnp.concatenate([part, part], axis=1)
        rows = slice(x * 32, (x + 1) * 32)
        for group in range(3):
            lanes = slice(group * 256, group * 256 + 256)
            value = keep_ref[x, :, lanes] + got_ref[rows, lanes]
            rows_ref[x, :, lanes] = count * value / (mine * sums[0:1, lanes])
        value = far_ref[rows, :] + far_got_ref[rows, :]
        rows_ref[x, :, 768:] = count * value / (mine * far_sums[0:1, :])


def scale(core, keep, got, own, far, far_got):
    return pl.pallas_call(
        scale_kernel,
        out_shape=jax.ShapeDtypeStruct((4, 32, 1024), jnp.float32),
        in_specs=[pl.BlockSpec(memory_space=pltpu.SMEM)] + [pl.BlockSpec(memory_space=pltpu.VMEM)] * 5,
        out_specs=pl.BlockSpec(memory_space=pltpu.VMEM),
        compiler_params=pltpu.CompilerParams(vmem_limit_bytes=8 << 20),
        name="scale",
    )(core, keep, got, own, far, far_got)


def place_kernel(at_ref, rows_ref, swap_ref, out_ref):
    core = at_ref[0]
    own, other = (pl.ds(pl.multiple_of(c * 32, 32), 32) for c in (core, 1 - core))
    for group in range(4):
        lanes = pl.ds(pl.multiple_of(at_ref[1 + group] * 256, 256), 256)
        source = slice(group * 256, (group + 1) * 256)
        for b in range(2):
            out_ref[b, own, lanes] = rows_ref[2 * core + b, :, source]
            out_ref[b, other, lanes] = swap_ref[b, :, source]


def place(at, rows, swap):
    return pl.pallas_call(
        place_kernel,
        out_shape=jax.ShapeDtypeStruct((2, 64, 1024), jnp.float32),
        in_specs=[pl.BlockSpec(memory_space=pltpu.SMEM)] + [pl.BlockSpec(memory_space=pltpu.VMEM)] * 2,
        out_specs=pl.BlockSpec(memory_space=pltpu.VMEM),
        compiler_params=pltpu.CompilerParams(vmem_limit_bytes=8 << 20),
        name="place",
    )(at, rows, swap)


SWAP = [(0, 1), (1, 0)]
NEAR = [(0, 1), (1, 0), (2, 3), (3, 2)]
WRAP = [(0, 3), (1, 2), (2, 1), (3, 0)]


def shards(raw_frames, eigen_flats, weights, flat_count, bin_map):
    core = lax.axis_index("c").astype(jnp.int32)
    row = lax.axis_index("y").astype(jnp.int32)
    packed = pack(weights.T, flat_count[None, :], bin_map.reshape(PIXELS // 128, 128), eigen_flats, raw_frames)
    mine = lax.all_to_all(packed, ("x", "z"), 0, 0, tiled=True).reshape(4 * DEPTH, 128)
    near = lax.ppermute(mine, "y", NEAR)
    wrap = lax.ppermute(mine, "y", WRAP)
    same, flip = cross(core[None], near, wrap)
    far_got = lax.ppermute(flip, ("c", "y"), [(4 * c + a, 4 * (1 - c) + b) for c in range(2) for a, b in NEAR])
    far = lax.ppermute(same, "y", NEAR)
    keep, send, own = gram(core[None], mine, near, wrap)
    got = lax.ppermute(send, "c", SWAP)
    at, second, rows = lax.optimization_barrier(
        (jnp.stack([core, row ^ 1, row, 3 - row, (row + 2) % 4]), 2 - 2 * core,
         scale(core[None], keep, got, own, far, far_got)))
    rows = lax.all_to_all(rows, "x", 0, 0, tiled=True)
    swap = lax.ppermute(lax.dynamic_slice_in_dim(rows, second, 2, 0, allow_negative_indices=False), "c", SWAP)
    return place(at, rows, swap)


def solution(mesh):
    split = Mesh(mesh.devices.reshape(16, 2, 4, 4), ("z", "c", "y", "x"))
    return jax.shard_map(
        shards,
        mesh=split,
        in_specs=(P(("y", "x"), ("z", "c")), P(None, ("z", "c")), P(("y", "x"), None), P(("y", "x")), P(("z", "c"))),
        out_specs=P(("z", "c"), ("y", "x"), None),
        check_vma=False,
    )
```

```python
import jax, jax.numpy as jnp
from jax import lax
from jax.experimental import pallas as pl
from jax.experimental.pallas import tpu as pltpu
from jax.sharding import Mesh, PartitionSpec as P

CAP = 96
FRAMES = 64
PIXELS = 8192
EIGEN = 16
BINS = 64
CHUNK = 256
CHUNKS = PIXELS // CHUNK
STEP = 512
STEPS = PIXELS // STEP
DEEP = 4
SLOTS = BINS * CAP
PART = CAP // 2
DESTS = 64
DEPTH = 16 * PART


def pack_kernel(weights_hbm, used_hbm, bins_hbm, eigen_hbm, raw_hbm, out_ref,
                weights_ref, used_ref, bins_ref, eigen_ref, raw_ref,
                hot_ref, cum_ref, row_ref, place0, place1, place2, place3, even_ref, odd_ref, slot_ref, sems):
    f32, bf16 = jnp.float32, jnp.bfloat16
    sources = (bins_hbm, eigen_hbm, weights_hbm, used_hbm, raw_hbm)
    targets = (bins_ref, eigen_ref, weights_ref, used_ref, raw_ref)
    loads = [pltpu.make_async_copy(a, b, sems.at[i]) for i, (a, b) in enumerate(zip(sources, targets))]
    for load in loads:
        load.start()
    zero = jnp.zeros((128, 128), f32)

    @pl.loop(0, SLOTS // 128)
    def _(i):
        slot_ref[pl.ds(pl.multiple_of(i * 128, 128), 128), :] = zero
    slot_ref[SLOTS:, :] = jnp.zeros((8, 128), f32)
    loads[0].wait()

    label = lax.broadcasted_iota(jnp.int32, (BINS, 128), 0) + 1
    for j in range(CHUNKS):
        for h in range(2):
            hot_ref[j * BINS:(j + 1) * BINS, h * 128:(h + 1) * 128] = jnp.where(
                bins_ref[2 * j + h:2 * j + h + 1, :] == label, 1.0, 0.0).astype(bf16)
    before = lax.broadcasted_iota(jnp.int32, (CHUNK, CHUNK + 128), 0)
    after = lax.broadcasted_iota(jnp.int32, (CHUNK, CHUNK + 128), 1)
    prefix = jnp.where((before < after) | (after >= CHUNK), 1.0, 0.0).astype(bf16)
    cum_ref[...] = jnp.dot(hot_ref[...], prefix, preferred_element_type=f32)
    carry = jnp.zeros((BINS, 128), f32)
    for j in range(CHUNKS):
        rows = slice(j * BINS, (j + 1) * BINS)
        for h in range(2):
            lanes = slice(h * 128, (h + 1) * 128)
            rank = jnp.sum(hot_ref[rows, lanes].astype(f32) * (cum_ref[rows, lanes] + carry), axis=0, keepdims=True)
            own = bins_ref[2 * j + h:2 * j + h + 1, :]
            row_ref[2 * j + h:2 * j + h + 1, :] = jnp.where(
                own > 0, (own - 1) * CAP + rank.astype(jnp.int32), SLOTS)
        carry = carry + cum_ref[rows, CHUNK:]
    places, values = (place0, place1, place2, place3), (even_ref, odd_ref)

    def fetch(j, k):
        rows = pl.ds(pl.multiple_of(j * (STEP // 128), STEP // 128), STEP // 128)
        return pltpu.make_async_copy(row_ref.at[rows, :], places[k], sems.at[5 + k])

    for k in range(DEEP):
        fetch(k, k).start()
    for load in loads[1:]:
        load.wait()

    in_use = lax.broadcasted_iota(jnp.int32, (EIGEN, FRAMES), 0) < used_ref[...]
    coef = jnp.where(in_use, weights_ref[...], 0.0)
    high = coef.astype(bf16)
    rest = coef - high.astype(f32)
    mid = rest.astype(bf16)
    low = (rest - mid.astype(f32)).astype(bf16)
    weights = jnp.concatenate([high.astype(f32), mid.astype(f32), low.astype(f32)], axis=0).T.astype(bf16)

    def correct(j, target):
        at = pl.ds(pl.multiple_of(j * STEP, STEP), STEP)
        flats = eigen_ref[:, at]
        field = 0.5 + jnp.dot(weights, jnp.concatenate([flats] * 3, axis=0), preferred_element_type=f32)
        value = (raw_ref[:, at].astype(f32) / field).astype(bf16).astype(f32)
        for h in range(STEP // 128):
            part = value[:, h * 128:(h + 1) * 128]
            target[h * 128:(h + 1) * 128, :] = jnp.concatenate([part, part], axis=0).T

    def scatter(source, place_ref):
        for i in range(STEP):
            slot_ref[pl.ds(place_ref[i // 128, i % 128], 1), :] = source[i:i + 1, :]

    correct(0, even_ref)

    @pl.loop(0, STEPS // DEEP)
    def _(i):
        for k in range(DEEP):
            fetch(DEEP * i + k, k).wait()
            scatter(values[k % 2], places[k])

            @pl.when(i < STEPS // DEEP - 1)
            def _():
                fetch(DEEP * (i + 1) + k, k).start()
            correct(jnp.minimum(DEEP * i + k + 1, STEPS - 1), values[(k + 1) % 2])

    left = lax.broadcasted_iota(jnp.int32, (PART, 128), 1) < FRAMES

    @pl.loop(0, BINS // 4)
    def _(z):
        for x in range(4):
            base = (4 * z + x) * CAP
            lo = slot_ref[pl.ds(pl.multiple_of(base, 8), PART), :]
            hi = slot_ref[pl.ds(pl.multiple_of(base + PART, 8), PART), :]
            out_ref[x * 16 + z] = jnp.where(left, lo, hi).astype(bf16)


def pack(weights, used, bins, eigen, raw):
    f32 = jnp.float32
    return pl.pallas_call(
        pack_kernel,
        out_shape=jax.ShapeDtypeStruct((DESTS, PART, 128), jnp.bfloat16),
        in_specs=[pl.BlockSpec(memory_space=pltpu.HBM)] * 5,
        out_specs=pl.BlockSpec(memory_space=pltpu.VMEM),
        scratch_shapes=[
            pltpu.VMEM((EIGEN, FRAMES), f32),
            pltpu.VMEM((1, FRAMES), jnp.int32),
            pltpu.VMEM((PIXELS // 128, 128), jnp.int32),
            pltpu.VMEM((EIGEN, PIXELS), jnp.bfloat16),
            pltpu.VMEM((FRAMES, PIXELS), jnp.bfloat16),
            pltpu.VMEM((CHUNKS * BINS, CHUNK), jnp.bfloat16),
            pltpu.VMEM((CHUNKS * BINS, CHUNK + 128), f32),
            pltpu.VMEM((PIXELS // 128, 128), jnp.int32),
            *[pltpu.SMEM((STEP // 128, 128), jnp.int32)] * DEEP,
            pltpu.VMEM((STEP, 128), f32),
            pltpu.VMEM((STEP, 128), f32),
            pltpu.VMEM((SLOTS + 8, 128), f32),
            pltpu.SemaphoreType.DMA((5 + DEEP,)),
        ],
        compiler_params=pltpu.CompilerParams(vmem_limit_bytes=24 << 20),
        name="pack",
    )(*(pltpu.with_memory_space_constraint(a, pltpu.HBM) for a in (weights, used, bins, eigen, raw)))


def matrix(ref):
    return jnp.concatenate([ref[x * DEPTH:(x + 1) * DEPTH, :] for x in range(4)], axis=1)


def fold(even_top, even_low, odd_top, odd_low):
    left = lax.broadcasted_iota(jnp.int32, (1, 128), 1) < FRAMES
    return jnp.where(left, even_top, odd_low) + pltpu.roll(
        jnp.where(left, odd_top, even_low), FRAMES, 1)


def products(full):
    for x in range(4):
        top, low = slice(x * 128, x * 128 + 64), slice(x * 128 + 64, x * 128 + 128)
        for e in range(2):
            even, odd = slice(e * 256, e * 256 + 128), slice(e * 256 + 128, e * 256 + 256)
            yield x, e, fold(full[top, even], full[low, even], full[top, odd], full[low, odd])


def totals(b):
    full = jnp.dot(jnp.ones((8, DEPTH), jnp.bfloat16), b, preferred_element_type=jnp.float32)
    for e in range(2):
        even, odd = full[:, e * 256:e * 256 + 128], full[:, e * 256 + 128:e * 256 + 256]
        yield e, fold(even, even, odd, odd)


def cross_kernel(core_ref, near_ref, wrap_ref, far_ref):
    first = core_ref[0] == 0
    near, wrap = matrix(near_ref), matrix(wrap_ref)
    full = lax.dot_general(near, wrap, (((0,), (0,)), ((), ())), preferred_element_type=jnp.float32)
    for x, e, part in products(full):
        lanes = slice(e * 128, e * 128 + 128)
        far_ref[0, x * 32:(x + 1) * 32, lanes] = jnp.where(first, part[:32], part[32:])
        far_ref[1, x * 32:(x + 1) * 32, lanes] = jnp.where(first, part[32:], part[:32])
    for e, part in totals(wrap):
        for half in range(2):
            far_ref[half, 128:, e * 128:e * 128 + 128] = part


def cross(core, near, wrap):
    return pl.pallas_call(
        cross_kernel,
        out_shape=jax.ShapeDtypeStruct((2, 136, 256), jnp.float32),
        in_specs=[pl.BlockSpec(memory_space=pltpu.SMEM)] + [pl.BlockSpec(memory_space=pltpu.VMEM)] * 2,
        out_specs=pl.BlockSpec(memory_space=pltpu.VMEM),
        compiler_params=pltpu.CompilerParams(vmem_limit_bytes=16 << 20),
        name="cross",
    )(core, near, wrap)


def self_kernel(core_ref, mine_ref, turned_ref, keep_ref, send_ref):
    f32, bf16 = jnp.float32, jnp.bfloat16
    first = core_ref[0] == 0
    mine = matrix(mine_ref)
    turned = mine.T
    turned_ref[...] = turned
    for x, e, part in products(jnp.dot(turned, mine, preferred_element_type=f32)):
        lanes = slice(e * 128, e * 128 + 128)
        keep_ref[x, :, lanes] = jnp.where(first, part[:32], part[32:])
        send_ref[x * 32:(x + 1) * 32, lanes] = jnp.where(first, part[32:], part[:32])
    for e, part in totals(mine):
        send_ref[128:136, e * 128:e * 128 + 128] = part
    hits = jnp.where(mine_ref[:DEPTH, :].astype(f32) != 0.0, 1.0, 0.0).astype(bf16)
    hits = jnp.dot(jnp.ones((8, DEPTH), bf16), hits, preferred_element_type=f32)
    hits = hits + pltpu.roll(hits, FRAMES, 1)
    send_ref[136:, :] = jnp.concatenate([hits, hits], axis=1)


def self_gram(core, mine):
    f32 = jnp.float32
    return pl.pallas_call(
        self_kernel,
        out_shape=(jax.ShapeDtypeStruct((512, DEPTH), jnp.bfloat16),
                   jax.ShapeDtypeStruct((4, 32, 256), f32),
                   jax.ShapeDtypeStruct((144, 256), f32)),
        in_specs=[pl.BlockSpec(memory_space=pltpu.SMEM), pl.BlockSpec(memory_space=pltpu.VMEM)],
        out_specs=(pl.BlockSpec(memory_space=pltpu.VMEM),) * 3,
        compiler_params=pltpu.CompilerParams(vmem_limit_bytes=16 << 20),
        name="self_gram",
    )(core, mine)


def gram_kernel(core_ref, turned_ref, near_ref, wrap_ref, self_keep_ref, self_send_ref, keep_ref, send_ref, own_ref):
    first = core_ref[0] == 0
    turned = turned_ref[...]
    for group, ref in ((0, near_ref), (2, wrap_ref)):
        other = matrix(ref)
        for x, e, part in products(jnp.dot(turned, other, preferred_element_type=jnp.float32)):
            lanes = slice(group * 256 + e * 128, group * 256 + e * 128 + 128)
            keep_ref[x, :, lanes] = jnp.where(first, part[:32], part[32:])
            send_ref[x * 32:(x + 1) * 32, lanes] = jnp.where(first, part[32:], part[:32])
        for e, part in totals(other):
            lanes = slice(group * 256 + e * 128, group * 256 + e * 128 + 128)
            own_ref[:8, lanes] = part
            send_ref[128:136, lanes] = part
    for x in range(4):
        keep_ref[x, :, 256:512] = self_keep_ref[x]
    send_ref[:136, 256:512] = self_send_ref[:136, :]
    own_ref[:8, 256:512] = self_send_ref[128:136, :]
    hits = jnp.concatenate([self_send_ref[136:, :]] * 3, axis=1)
    own_ref[8:, :] = hits
    send_ref[136:, :] = hits


def gram(core, turned, near, wrap, self_keep, self_send):
    f32 = jnp.float32
    return pl.pallas_call(
        gram_kernel,
        out_shape=(jax.ShapeDtypeStruct((4, 32, 768), f32),
                   jax.ShapeDtypeStruct((144, 768), f32),
                   jax.ShapeDtypeStruct((16, 768), f32)),
        in_specs=[pl.BlockSpec(memory_space=pltpu.SMEM)] + [pl.BlockSpec(memory_space=pltpu.VMEM)] * 5,
        out_specs=(pl.BlockSpec(memory_space=pltpu.VMEM),) * 3,
        compiler_params=pltpu.CompilerParams(vmem_limit_bytes=16 << 20),
        name="gram",
    )(core, turned, near, wrap, self_keep, self_send)


def scale_kernel(core_ref, keep_ref, got_ref, own_ref, far_ref, far_got_ref, rows_ref):
    first = core_ref[0] == 0
    sums = own_ref[...] + got_ref[128:, :]
    far_sums = far_ref[0, 128:, :] + far_got_ref[128:, :]
    count = sums[8:9, :256]
    tall = [jnp.broadcast_to(sums[0:1, 256 + e * 128:384 + e * 128], (128, 128)).T for e in range(2)]
    tall = jnp.concatenate(tall, axis=0)
    for x in range(4):
        part = jnp.where(first, tall[x * 64:x * 64 + 32], tall[x * 64 + 32:x * 64 + 64])
        mine = jnp.concatenate([part, part], axis=1)
        rows = slice(x * 32, (x + 1) * 32)
        for group in range(3):
            lanes = slice(group * 256, group * 256 + 256)
            value = keep_ref[x, :, lanes] + got_ref[rows, lanes]
            rows_ref[x, :, lanes] = count * value / (mine * sums[0:1, lanes])
        value = far_ref[0, rows, :] + far_got_ref[rows, :]
        rows_ref[x, :, 768:] = count * value / (mine * far_sums[0:1, :])


def scale(core, keep, got, own, far, far_got):
    return pl.pallas_call(
        scale_kernel,
        out_shape=jax.ShapeDtypeStruct((4, 32, 1024), jnp.float32),
        in_specs=[pl.BlockSpec(memory_space=pltpu.SMEM)] + [pl.BlockSpec(memory_space=pltpu.VMEM)] * 5,
        out_specs=pl.BlockSpec(memory_space=pltpu.VMEM),
        compiler_params=pltpu.CompilerParams(vmem_limit_bytes=8 << 20),
        name="scale",
    )(core, keep, got, own, far, far_got)


def place_kernel(at_ref, rows_ref, swap_ref, out_ref):
    core = at_ref[0]
    own, other = (pl.ds(pl.multiple_of(c * 32, 32), 32) for c in (core, 1 - core))
    for group in range(4):
        lanes = pl.ds(pl.multiple_of(at_ref[1 + group] * 256, 256), 256)
        source = slice(group * 256, (group + 1) * 256)
        for b in range(2):
            out_ref[b, own, lanes] = rows_ref[2 * core + b, :, source]
            out_ref[b, other, lanes] = swap_ref[b, :, source]


def place(at, rows, swap):
    return pl.pallas_call(
        place_kernel,
        out_shape=jax.ShapeDtypeStruct((2, 64, 1024), jnp.float32),
        in_specs=[pl.BlockSpec(memory_space=pltpu.SMEM)] + [pl.BlockSpec(memory_space=pltpu.VMEM)] * 2,
        out_specs=pl.BlockSpec(memory_space=pltpu.VMEM),
        compiler_params=pltpu.CompilerParams(vmem_limit_bytes=8 << 20),
        name="place",
    )(at, rows, swap)


SWAP = [(0, 1), (1, 0)]
NEAR = [(0, 1), (1, 0), (2, 3), (3, 2)]
WRAP = [(0, 3), (1, 2), (2, 1), (3, 0)]


def shards(raw_frames, eigen_flats, weights, flat_count, bin_map):
    core = lax.axis_index("c").astype(jnp.int32)
    row = lax.axis_index("y").astype(jnp.int32)
    packed = pack(weights.T, flat_count[None, :], bin_map.reshape(PIXELS // 128, 128), eigen_flats, raw_frames)
    mine = lax.all_to_all(packed, ("x", "z"), 0, 0, tiled=True).reshape(4 * DEPTH, 128)
    near = lax.ppermute(mine, "y", NEAR)
    wrap = lax.ppermute(mine, "y", WRAP)
    turned, self_keep, self_send = self_gram(core[None], mine)
    far = lax.ppermute(cross(core[None], near, wrap), "y", NEAR)
    keep, send, own = gram(core[None], turned, near, wrap, self_keep, self_send)
    got = lax.ppermute(send, "c", SWAP)
    far_got = lax.ppermute(far[1], "c", SWAP)
    at, second, rows = lax.optimization_barrier(
        (jnp.stack([core, row ^ 1, row, 3 - row, (row + 2) % 4]), 2 - 2 * core,
         scale(core[None], keep, got, own, far, far_got)))
    rows = lax.all_to_all(rows, "x", 0, 0, tiled=True)
    swap = lax.ppermute(lax.dynamic_slice_in_dim(rows, second, 2, 0, allow_negative_indices=False), "c", SWAP)
    return place(at, rows, swap)


def solution(mesh):
    split = Mesh(mesh.devices.reshape(16, 2, 4, 4), ("z", "c", "y", "x"))
    return jax.shard_map(
        shards,
        mesh=split,
        in_specs=(P(("y", "x"), ("z", "c")), P(None, ("z", "c")), P(("y", "x"), None), P(("y", "x")), P(("z", "c"))),
        out_specs=P(("z", "c"), ("y", "x"), None),
        check_vma=False,
    )
```

```python
import jax, jax.numpy as jnp
from jax import lax
from jax.experimental import pallas as pl
from jax.experimental.pallas import tpu as pltpu
from jax.sharding import Mesh, PartitionSpec as P

CAP = 96
FRAMES = 64
PIXELS = 8192
EIGEN = 16
BINS = 64
CHUNK = 256
CHUNKS = PIXELS // CHUNK
STEP = 512
STEPS = PIXELS // STEP
DEEP = 4
SLOTS = BINS * CAP
PART = CAP // 2
DESTS = 64
DEPTH = 16 * PART


def pack_kernel(weights_hbm, used_hbm, bins_hbm, eigen_hbm, raw_hbm, out_ref,
                weights_ref, used_ref, bins_ref, eigen_ref, raw_ref,
                hot_ref, cum_ref, row_ref, place0, place1, place2, place3, even_ref, odd_ref, slot_ref, sems):
    f32, bf16 = jnp.float32, jnp.bfloat16
    sources = (bins_hbm, eigen_hbm, weights_hbm, used_hbm, raw_hbm)
    targets = (bins_ref, eigen_ref, weights_ref, used_ref, raw_ref)
    loads = [pltpu.make_async_copy(a, b, sems.at[i]) for i, (a, b) in enumerate(zip(sources, targets))]
    for load in loads:
        load.start()
    zero = jnp.zeros((128, 128), f32)

    @pl.loop(0, SLOTS // 128)
    def _(i):
        slot_ref[pl.ds(pl.multiple_of(i * 128, 128), 128), :] = zero
    slot_ref[SLOTS:, :] = jnp.zeros((8, 128), f32)
    loads[0].wait()

    label = lax.broadcasted_iota(jnp.int32, (BINS, 128), 0) + 1
    for j in range(CHUNKS):
        for h in range(2):
            hot_ref[j * BINS:(j + 1) * BINS, h * 128:(h + 1) * 128] = jnp.where(
                bins_ref[2 * j + h:2 * j + h + 1, :] == label, 1.0, 0.0).astype(bf16)
    before = lax.broadcasted_iota(jnp.int32, (CHUNK, CHUNK + 128), 0)
    after = lax.broadcasted_iota(jnp.int32, (CHUNK, CHUNK + 128), 1)
    prefix = jnp.where((before < after) | (after >= CHUNK), 1.0, 0.0).astype(bf16)
    cum_ref[...] = jnp.dot(hot_ref[...], prefix, preferred_element_type=f32)
    carry = jnp.zeros((BINS, 128), f32)
    for j in range(CHUNKS):
        rows = slice(j * BINS, (j + 1) * BINS)
        for h in range(2):
            lanes = slice(h * 128, (h + 1) * 128)
            rank = jnp.sum(hot_ref[rows, lanes].astype(f32) * (cum_ref[rows, lanes] + carry), axis=0, keepdims=True)
            own = bins_ref[2 * j + h:2 * j + h + 1, :]
            row_ref[2 * j + h:2 * j + h + 1, :] = jnp.where(
                own > 0, (own - 1) * CAP + rank.astype(jnp.int32), SLOTS)
        carry = carry + cum_ref[rows, CHUNK:]
    places, values = (place0, place1, place2, place3), (even_ref, odd_ref)

    def fetch(j, k):
        rows = pl.ds(pl.multiple_of(j * (STEP // 128), STEP // 128), STEP // 128)
        return pltpu.make_async_copy(row_ref.at[rows, :], places[k], sems.at[5 + k])

    for k in range(DEEP):
        fetch(k, k).start()
    for load in loads[1:]:
        load.wait()

    in_use = lax.broadcasted_iota(jnp.int32, (EIGEN, FRAMES), 0) < used_ref[...]
    coef = jnp.where(in_use, weights_ref[...], 0.0)
    high = coef.astype(bf16)
    rest = coef - high.astype(f32)
    mid = rest.astype(bf16)
    low = (rest - mid.astype(f32)).astype(bf16)
    weights = jnp.concatenate([high.astype(f32), mid.astype(f32), low.astype(f32)], axis=0).T.astype(bf16)

    def correct(j, target):
        at = pl.ds(pl.multiple_of(j * STEP, STEP), STEP)
        flats = eigen_ref[:, at]
        field = 0.5 + jnp.dot(weights, jnp.concatenate([flats] * 3, axis=0), preferred_element_type=f32)
        value = (raw_ref[:, at].astype(f32) / field).astype(bf16).astype(f32)
        for h in range(STEP // 128):
            part = value[:, h * 128:(h + 1) * 128]
            target[h * 128:(h + 1) * 128, :] = jnp.concatenate([part, part], axis=0).T

    def scatter(source, place_ref):
        for i in range(STEP):
            slot_ref[pl.ds(place_ref[i // 128, i % 128], 1), :] = source[i:i + 1, :]

    correct(0, even_ref)

    @pl.loop(0, STEPS // DEEP)
    def _(i):
        for k in range(DEEP):
            fetch(DEEP * i + k, k).wait()
            scatter(values[k % 2], places[k])

            @pl.when(i < STEPS // DEEP - 1)
            def _():
                fetch(DEEP * (i + 1) + k, k).start()
            correct(jnp.minimum(DEEP * i + k + 1, STEPS - 1), values[(k + 1) % 2])

    left = lax.broadcasted_iota(jnp.int32, (PART, 128), 1) < FRAMES

    @pl.loop(0, BINS // 4)
    def _(z):
        for x in range(4):
            base = (4 * z + x) * CAP
            lo = slot_ref[pl.ds(pl.multiple_of(base, 8), PART), :]
            hi = slot_ref[pl.ds(pl.multiple_of(base + PART, 8), PART), :]
            out_ref[x * 16 + z] = jnp.where(left, lo, hi).astype(bf16)


def pack(weights, used, bins, eigen, raw):
    f32 = jnp.float32
    return pl.pallas_call(
        pack_kernel,
        out_shape=jax.ShapeDtypeStruct((DESTS, PART, 128), jnp.bfloat16),
        in_specs=[pl.BlockSpec(memory_space=pltpu.HBM)] * 5,
        out_specs=pl.BlockSpec(memory_space=pltpu.VMEM),
        scratch_shapes=[
            pltpu.VMEM((EIGEN, FRAMES), f32),
            pltpu.VMEM((1, FRAMES), jnp.int32),
            pltpu.VMEM((PIXELS // 128, 128), jnp.int32),
            pltpu.VMEM((EIGEN, PIXELS), jnp.bfloat16),
            pltpu.VMEM((FRAMES, PIXELS), jnp.bfloat16),
            pltpu.VMEM((CHUNKS * BINS, CHUNK), jnp.bfloat16),
            pltpu.VMEM((CHUNKS * BINS, CHUNK + 128), f32),
            pltpu.VMEM((PIXELS // 128, 128), jnp.int32),
            *[pltpu.SMEM((STEP // 128, 128), jnp.int32)] * DEEP,
            pltpu.VMEM((STEP, 128), f32),
            pltpu.VMEM((STEP, 128), f32),
            pltpu.VMEM((SLOTS + 8, 128), f32),
            pltpu.SemaphoreType.DMA((5 + DEEP,)),
        ],
        compiler_params=pltpu.CompilerParams(vmem_limit_bytes=24 << 20),
        name="pack",
    )(*(pltpu.with_memory_space_constraint(a, pltpu.HBM) for a in (weights, used, bins, eigen, raw)))


def matrix(ref):
    return jnp.concatenate([ref[x * DEPTH:(x + 1) * DEPTH, :] for x in range(4)], axis=1)


def fold(even_top, even_low, odd_top, odd_low):
    left = lax.broadcasted_iota(jnp.int32, (1, 128), 1) < FRAMES
    return jnp.where(left, even_top, odd_low) + pltpu.roll(
        jnp.where(left, odd_top, even_low), FRAMES, 1)


def products(a, b):
    full = lax.dot_general(a, b, (((0,), (0,)), ((), ())), preferred_element_type=jnp.float32)
    for x in range(4):
        top, low = slice(x * 128, x * 128 + 64), slice(x * 128 + 64, x * 128 + 128)
        for e in range(2):
            even, odd = slice(e * 256, e * 256 + 128), slice(e * 256 + 128, e * 256 + 256)
            yield x, e, fold(full[top, even], full[low, even], full[top, odd], full[low, odd])


def totals(b):
    full = jnp.dot(jnp.ones((8, DEPTH), jnp.bfloat16), b, preferred_element_type=jnp.float32)
    for e in range(2):
        even, odd = full[:, e * 256:e * 256 + 128], full[:, e * 256 + 128:e * 256 + 256]
        yield e, fold(even, even, odd, odd)


def cross_kernel(core_ref, near_ref, wrap_ref, far_ref):
    first = core_ref[0] == 0
    near, wrap = matrix(near_ref), matrix(wrap_ref)
    for x, e, part in products(near, wrap):
        lanes = slice(e * 128, e * 128 + 128)
        far_ref[0, x * 32:(x + 1) * 32, lanes] = jnp.where(first, part[:32], part[32:])
        far_ref[1, x * 32:(x + 1) * 32, lanes] = jnp.where(first, part[32:], part[:32])
    for e, part in totals(wrap):
        for half in range(2):
            far_ref[half, 128:, e * 128:e * 128 + 128] = part


def cross(core, near, wrap):
    return pl.pallas_call(
        cross_kernel,
        out_shape=jax.ShapeDtypeStruct((2, 136, 256), jnp.float32),
        in_specs=[pl.BlockSpec(memory_space=pltpu.SMEM)] + [pl.BlockSpec(memory_space=pltpu.VMEM)] * 2,
        out_specs=pl.BlockSpec(memory_space=pltpu.VMEM),
        compiler_params=pltpu.CompilerParams(vmem_limit_bytes=16 << 20),
        name="cross",
    )(core, near, wrap)


def gram_kernel(core_ref, mine_ref, near_ref, wrap_ref, keep_ref, send_ref, own_ref):
    f32, bf16 = jnp.float32, jnp.bfloat16
    first = core_ref[0] == 0
    mine = matrix(mine_ref)
    for group, ref in enumerate((near_ref, mine_ref, wrap_ref)):
        other = matrix(ref)
        for x, e, part in products(mine, other):
            lanes = slice(group * 256 + e * 128, group * 256 + e * 128 + 128)
            keep_ref[x, :, lanes] = jnp.where(first, part[:32], part[32:])
            send_ref[x * 32:(x + 1) * 32, lanes] = jnp.where(first, part[32:], part[:32])
        for e, part in totals(other):
            lanes = slice(group * 256 + e * 128, group * 256 + e * 128 + 128)
            own_ref[:8, lanes] = part
            send_ref[128:136, lanes] = part
    hits = jnp.where(mine_ref[:DEPTH, :].astype(f32) != 0.0, 1.0, 0.0).astype(bf16)
    hits = jnp.dot(jnp.ones((8, DEPTH), bf16), hits, preferred_element_type=f32)
    hits = hits + pltpu.roll(hits, FRAMES, 1)
    hits = jnp.concatenate([hits] * 6, axis=1)
    own_ref[8:, :] = hits
    send_ref[136:, :] = hits


def gram(core, mine, near, wrap):
    f32 = jnp.float32
    return pl.pallas_call(
        gram_kernel,
        out_shape=(jax.ShapeDtypeStruct((4, 32, 768), f32),
                   jax.ShapeDtypeStruct((144, 768), f32),
                   jax.ShapeDtypeStruct((16, 768), f32)),
        in_specs=[pl.BlockSpec(memory_space=pltpu.SMEM)] + [pl.BlockSpec(memory_space=pltpu.VMEM)] * 3,
        out_specs=(pl.BlockSpec(memory_space=pltpu.VMEM),) * 3,
        compiler_params=pltpu.CompilerParams(vmem_limit_bytes=24 << 20),
        name="gram",
    )(core, mine, near, wrap)


def scale_kernel(core_ref, keep_ref, got_ref, own_ref, far_ref, far_got_ref, rows_ref):
    first = core_ref[0] == 0
    sums = own_ref[...] + got_ref[128:, :]
    far_sums = far_ref[0, 128:, :] + far_got_ref[128:, :]
    count = sums[8:9, :256]
    tall = [jnp.broadcast_to(sums[0:1, 256 + e * 128:384 + e * 128], (128, 128)).T for e in range(2)]
    tall = jnp.concatenate(tall, axis=0)
    for x in range(4):
        part = jnp.where(first, tall[x * 64:x * 64 + 32], tall[x * 64 + 32:x * 64 + 64])
        mine = jnp.concatenate([part, part], axis=1)
        rows = slice(x * 32, (x + 1) * 32)
        for group in range(3):
            lanes = slice(group * 256, group * 256 + 256)
            value = keep_ref[x, :, lanes] + got_ref[rows, lanes]
            rows_ref[x, :, lanes] = count * value / (mine * sums[0:1, lanes])
        value = far_ref[0, rows, :] + far_got_ref[rows, :]
        rows_ref[x, :, 768:] = count * value / (mine * far_sums[0:1, :])


def scale(core, keep, got, own, far, far_got):
    return pl.pallas_call(
        scale_kernel,
        out_shape=jax.ShapeDtypeStruct((4, 32, 1024), jnp.float32),
        in_specs=[pl.BlockSpec(memory_space=pltpu.SMEM)] + [pl.BlockSpec(memory_space=pltpu.VMEM)] * 5,
        out_specs=pl.BlockSpec(memory_space=pltpu.VMEM),
        compiler_params=pltpu.CompilerParams(vmem_limit_bytes=8 << 20),
        name="scale",
    )(core, keep, got, own, far, far_got)


def copy_rows(at_ref, source_ref, first, half, out_ref, sems):
    copies = []
    for b in range(2):
        for group in range(4):
            lanes = pl.ds(pl.multiple_of(at_ref[1 + group] * 256, 256), 256)
            rows = pl.ds(pl.multiple_of(half * 32, 32), 32)
            copies.append(pltpu.make_async_copy(
                source_ref.at[first + b, :, group * 256:(group + 1) * 256],
                out_ref.at[b, rows, lanes], sems.at[4 * b + group]))
    for copy in copies:
        copy.start()
    for copy in copies:
        copy.wait()


def own_kernel(at_ref, rows_ref, out_ref, sems):
    copy_rows(at_ref, rows_ref, 2 * at_ref[0], at_ref[0], out_ref, sems)


def other_kernel(at_ref, swap_ref, half_ref, out_ref, sems):
    copy_rows(at_ref, swap_ref, 0, 1 - at_ref[0], out_ref, sems)


def place(at, rows, swap):
    smem, vmem, hbm = (pl.BlockSpec(memory_space=m) for m in (pltpu.SMEM, pltpu.VMEM, pltpu.HBM))
    shape = jax.ShapeDtypeStruct((2, 64, 1024), jnp.float32)
    sems = [pltpu.SemaphoreType.DMA((8,))]
    params = pltpu.CompilerParams(vmem_limit_bytes=8 << 20)
    half = pl.pallas_call(own_kernel, out_shape=shape, in_specs=[smem, vmem], out_specs=hbm,
                          scratch_shapes=sems, compiler_params=params, name="own_rows")(at, rows)
    return pl.pallas_call(other_kernel, out_shape=shape, in_specs=[smem, vmem, hbm], out_specs=hbm,
                          scratch_shapes=sems, compiler_params=params, name="other_rows",
                          input_output_aliases={2: 0})(at, swap, half)


SWAP = [(0, 1), (1, 0)]
NEAR = [(0, 1), (1, 0), (2, 3), (3, 2)]
WRAP = [(0, 3), (1, 2), (2, 1), (3, 0)]


def shards(raw_frames, eigen_flats, weights, flat_count, bin_map):
    core = lax.axis_index("c").astype(jnp.int32)
    row = lax.axis_index("y").astype(jnp.int32)
    packed = pack(weights.T, flat_count[None, :], bin_map.reshape(PIXELS // 128, 128), eigen_flats, raw_frames)
    mine = lax.all_to_all(packed, ("x", "z"), 0, 0, tiled=True).reshape(4 * DEPTH, 128)
    near = lax.ppermute(mine, "y", NEAR)
    wrap = lax.ppermute(mine, "y", WRAP)
    far = lax.ppermute(cross(core[None], near, wrap), "y", NEAR)
    keep, send, own = gram(core[None], mine, near, wrap)
    got = lax.ppermute(send, "c", SWAP)
    far_got = lax.ppermute(far[1], "c", SWAP)
    at, second, rows = lax.optimization_barrier(
        (jnp.stack([core, row ^ 1, row, 3 - row, (row + 2) % 4]), 2 - 2 * core,
         scale(core[None], keep, got, own, far, far_got)))
    rows = lax.all_to_all(rows, "x", 0, 0, tiled=True)
    swap = lax.ppermute(lax.dynamic_slice_in_dim(rows, second, 2, 0, allow_negative_indices=False), "c", SWAP)
    return place(at, rows, swap)


def solution(mesh):
    split = Mesh(mesh.devices.reshape(16, 2, 4, 4), ("z", "c", "y", "x"))
    return jax.shard_map(
        shards,
        mesh=split,
        in_specs=(P(("y", "x"), ("z", "c")), P(None, ("z", "c")), P(("y", "x"), None), P(("y", "x")), P(("z", "c"))),
        out_specs=P(("z", "c"), ("y", "x"), None),
        check_vma=False,
    )
```
